512 devices in a mesh: slab: 128 (over z, y, core), col: 4 (over x).
Axes of the slice: x: 4, y: 8, z: 8, core: 2. Of those that a mesh axis runs over, the one named last changes fastest.
Arguments:
- shot_boxes: int32 [4, 131072], P(None, ('slab', 'col')), may hold values from 0 to 8192, as said below
- shot_counts: int32 [128, 4], P('slab', 'col'), may hold values from 128 to 256, as said below
- shot_doses: float32 [131072], P(('slab', 'col')), may hold values from 0.2 to 1
- transfer: float32 [4096, 4096], P(('slab', 'col')), may hold values from 0.2 to 1
Outputs:
- dosage: float32 [131072], P(('slab', 'col'))
- exposure: float32 [8192, 8192], P('slab', 'col')
The draws below stay inside these ranges and needn't reach their ends.
Inputs may be any that keep to these rules, and one draw needn't show every extreme that they name: `shot_boxes`: rows 0 to 3 hold a shot's first row, end row, first column and end column (ends exclusive); every shot covers one pixel or more. Slots are owned in blocks of 256 along slab+col; a shot's first row lies in its owner's 64 rows, its end row at most 64 rows further and never past the grid; its columns lie in its owner's 2048 columns, 64 at most. `shot_counts`: the first that many slots of each device are live, a multiple of 32; some device has all 256 live in every draw.
All inputs are finite; a program needn't handle non-finite values.
Results may differ from the reference program's by a relative error of at most 0.0023.
Values may be sent and summed in bfloat16 or wider, within the bound.
A program may use at most 128 MiB of HBM per device.

```python
import math
import jax
import jax.numpy as jnp
from jax import lax

POOL = 2
HALO = 64
CAP = 256
ITERS = 2
TILE_ROWS = 64
TILE_COLS = 2048
FINE_ROWS = 8192
FINE_COLS = 8192
NCR = 4096
NCC = 4096
SHOTS = 131072
N_SLAB = 128
N_COL = 4


def draw_shot_counts(key, part):
    first = jax.random.randint(jax.random.fold_in(key, 11), (N_SLAB * N_COL,), 0, 8)
    second = jax.random.randint(jax.random.fold_in(key, 12), (N_SLAB * N_COL,), 0, 8)
    levels = jnp.minimum(8, 4 + first * second // 12)
    chosen = jax.random.randint(jax.random.fold_in(key, 13), (), 0, N_SLAB * N_COL)
    levels = jnp.where(jnp.arange(N_SLAB * N_COL, dtype=jnp.int32) == chosen, 8, levels)
    return (CAP * levels // 8).reshape(N_SLAB, N_COL).astype(jnp.int32)


def draw_shot_boxes(key, part):
    number = CAP * N_SLAB * N_COL
    slot_ids = jnp.arange(number, dtype=jnp.int32)
    owner = slot_ids // CAP
    slab_pos = owner // N_COL
    col_pos = owner % N_COL
    start_row = slab_pos * TILE_ROWS + jax.random.randint(jax.random.fold_in(key, 21), (number,), 0, TILE_ROWS)
    height = jax.random.randint(jax.random.fold_in(key, 22), (number,), 1, TILE_ROWS + 1)
    end_row = jnp.minimum(start_row + height, TILE_ROWS * N_SLAB)
    widest = min(64, TILE_COLS)
    width = jax.random.randint(jax.random.fold_in(key, 23), (number,), 1, widest + 1)
    shift_col = jax.random.randint(jax.random.fold_in(key, 24), (number,), 0, TILE_COLS - width + 1)
    start_col = col_pos * TILE_COLS + shift_col
    return jnp.stack([start_row, end_row, start_col, start_col + width]).astype(jnp.int32)


def level_of(key, shape, shards, smallest, top_value):
    def one(axis_at, shards_of):
        steps = jax.random.uniform(jax.random.fold_in(jax.random.fold_in(key, 6), axis_at), (shards_of,), jnp.float32, smallest / len(shards), top_value / len(shards))
        return jnp.repeat(jnp.exp(steps), shape[axis_at] // shards_of).reshape((-1,) + (1,) * (len(shape) - axis_at - 1))

    factor_of = one(*shards[0])
    for cut in shards[1:]:
        factor_of = factor_of * one(*cut)
    return factor_of


def setup_inputs(seed: int = 0) -> dict:
    splits = jax.random.split(jax.random.key(seed), 5)
    shot_boxes = draw_shot_boxes(jax.random.fold_in(splits[4], 71), 0)
    shot_counts = draw_shot_counts(jax.random.fold_in(splits[4], 71), 0)
    shot_doses = jnp.clip(jnp.exp(math.log(1.0) - 1.609438 * jax.random.uniform(splits[2], (SHOTS,), jnp.float32) ** level_of(splits[2], (SHOTS,), ((0, 512),), -0.2, 0.2)), 0.2, 1.0)
    transfer = jnp.clip(0.2 + 0.8 * jax.random.uniform(splits[3], (NCC, NCR), jnp.float32) ** level_of(splits[3], (NCC, NCR), ((0, 512),), -0.2, 0.2), 0.2, 1.0)
    return dict(shot_boxes=shot_boxes, shot_counts=shot_counts, shot_doses=shot_doses, transfer=transfer)


RELAX = 0.5
TARGET_LEVEL = 1.0


def band_matrix(number):
    row_pos = lax.broadcasted_iota(jnp.int32, (number, number + 2 * HALO), 0)
    col_pos = lax.broadcasted_iota(jnp.int32, (number, number + 2 * HALO), 1)
    offset = col_pos - row_pos
    spread = HALO / 3.0
    tap_pos = jnp.arange(-HALO, HALO + 1).astype(jnp.float32)
    tap_sum = jnp.sum(jnp.exp(-0.5 * tap_pos * tap_pos / (spread * spread)))
    centred = (offset - HALO).astype(jnp.float32)
    values = jnp.exp(-0.5 * centred * centred / (spread * spread)) / tap_sum
    inside = (offset >= 0) & (offset <= 2 * HALO)
    return jnp.where(inside, values, jnp.float32(0.0)).astype(jnp.bfloat16)


def covers(shot_box, row_start, col_start):
    number = shot_box.shape[1]
    row_pos = row_start + lax.broadcasted_iota(jnp.int32, (TILE_ROWS, number), 0)
    row_cover = ((row_pos >= shot_box[0][None, :]) & (row_pos < shot_box[1][None, :])).astype(jnp.bfloat16)
    col_pos = col_start + lax.broadcasted_iota(jnp.int32, (number, TILE_COLS), 1)
    col_cover = ((col_pos >= shot_box[2][:, None]) & (col_pos < shot_box[3][:, None])).astype(jnp.bfloat16)
    return row_cover, col_cover


def short_blur(raster_bf):
    rows_band = band_matrix(TILE_ROWS)
    padded = jnp.pad(raster_bf, ((HALO, HALO), (0, 0)))

    def row_pass(position):
        window = lax.dynamic_slice_in_dim(padded, position * TILE_ROWS, TILE_ROWS + 2 * HALO, 0)
        return jnp.dot(rows_band, window, preferred_element_type=jnp.float32).astype(jnp.bfloat16)

    middle = lax.map(row_pass, jnp.arange(N_SLAB, dtype=jnp.int32)).reshape(FINE_ROWS, FINE_COLS)
    cols_band = band_matrix(128).T
    widened = jnp.pad(middle, ((0, 0), (HALO, HALO)))

    def col_pass(position):
        window = lax.dynamic_slice_in_dim(widened, position * 128, 128 + 2 * HALO, 1)
        return jnp.dot(window, cols_band, preferred_element_type=jnp.float32)

    pieces = lax.map(col_pass, jnp.arange(FINE_COLS // 128, dtype=jnp.int32))
    return pieces.transpose(1, 0, 2).reshape(FINE_ROWS, FINE_COLS)


def reference(shot_boxes, shot_counts, shot_doses, transfer):
    devices_all = N_SLAB * N_COL
    box_grid = shot_boxes.reshape(4, N_SLAB, N_COL, CAP)
    upper_boxes = jnp.concatenate([jnp.zeros_like(box_grid[:, :1]), box_grid[:, :-1]], axis=1)
    tile_boxes = jnp.concatenate([box_grid, upper_boxes], axis=3).reshape(4, devices_all, 2 * CAP).transpose(1, 0, 2)
    slot_ids = jnp.arange(CAP, dtype=jnp.int32)
    live_slot = slot_ids[None, None, :] < shot_counts[:, :, None]
    dosage = jnp.where(live_slot, shot_doses.reshape(N_SLAB, N_COL, CAP), jnp.float32(0.0))
    shot_area = ((box_grid[1] - box_grid[0]) * (box_grid[3] - box_grid[2])).astype(jnp.float32)
    device_ids = jnp.arange(devices_all, dtype=jnp.int32)
    row_starts = (device_ids // N_COL) * TILE_ROWS
    col_starts = (device_ids % N_COL) * TILE_COLS

    def paint_tile(member):
        shot_box, weights, row_start, col_start = member
        row_cover, col_cover = covers(shot_box, row_start, col_start)
        return jnp.dot(row_cover, col_cover * weights[:, None], preferred_element_type=jnp.float32)

    def measure(member):
        shot_box, tile_exposure, row_start, col_start = member
        row_cover, col_cover = covers(shot_box, row_start, col_start)
        covered = jnp.dot(row_cover.T, tile_exposure, preferred_element_type=jnp.float32)
        return jnp.sum(covered * col_cover.astype(jnp.float32), axis=1)

    for iteration in range(ITERS):
        dosage_bf = dosage.astype(jnp.bfloat16)
        upper_doses = jnp.concatenate([jnp.zeros_like(dosage_bf[:1]), dosage_bf[:-1]], axis=0)
        weights = jnp.concatenate([dosage_bf, upper_doses], axis=2).reshape(devices_all, 2 * CAP)
        raster_tiles = lax.map(paint_tile, (tile_boxes, weights, row_starts, col_starts))
        raster = raster_tiles.reshape(N_SLAB, N_COL, TILE_ROWS, TILE_COLS).transpose(0, 2, 1, 3).reshape(FINE_ROWS, FINE_COLS)
        short_range = short_blur(raster.astype(jnp.bfloat16))
        coarse = raster.reshape(NCR, POOL, NCC, POOL).mean(axis=(1, 3))
        spectrum = jnp.fft.fft2(coarse) * transfer.T
        backscatter = jnp.fft.ifft2(spectrum).real
        upsampled = jnp.repeat(jnp.repeat(backscatter, POOL, axis=0), POOL, axis=1)
        exposure = short_range + upsampled
        exposure_tiles = exposure.astype(jnp.bfloat16).reshape(N_SLAB, TILE_ROWS, N_COL, TILE_COLS).transpose(0, 2, 1, 3).reshape(devices_all, TILE_ROWS, TILE_COLS)
        partial_value = lax.map(measure, (tile_boxes, exposure_tiles, row_starts, col_starts)).reshape(N_SLAB, N_COL, 2 * CAP)
        returned = jnp.concatenate([partial_value[1:, :, CAP:], jnp.zeros((1, N_COL, CAP), jnp.float32)], axis=0)
        average = (partial_value[:, :, :CAP] + returned) / shot_area
        dosage = jnp.where(live_slot, dosage * jnp.exp(RELAX * (TARGET_LEVEL - average)), jnp.float32(0.0))
    return dosage.reshape(SHOTS), exposure
```

```python
import functools

import jax
import jax.numpy as jnp
import numpy as np
from jax import lax
from jax.experimental import pallas as pl
from jax.experimental.pallas import tpu as pltpu
from jax.sharding import PartitionSpec as P

HALO = 64
ITERS = 2
SLOTS = 256
ROWS = 64
COLS = 2048
LONG = 4096
NZ = 8
NYC = 16
N_SLAB = NZ * NYC
N_COL = 4
RELAX = 0.5
TARGET_LEVEL = 1.0
F32 = jnp.float32
BF16 = jnp.bfloat16
MESH = pl.DeviceIdType.MESH


def halves(values):
    high = np.asarray(values, np.float32).astype(jnp.bfloat16)
    low = (np.asarray(values, np.float64) - high.astype(np.float64)).astype(jnp.bfloat16)
    return high, low


def blur_taps():
    pos = np.arange(-HALO, HALO + 1).astype(np.float32)
    spread = np.float32(HALO / 3.0)
    raw = np.exp(np.float32(-0.5) * pos * pos / (spread * spread)).astype(np.float32)
    return (raw / raw.sum(dtype=np.float32)).astype(jnp.bfloat16)


@functools.lru_cache(None)
def tables():
    turn = 2.0 * np.pi
    yc, z, mm = np.meshgrid(np.arange(NYC), np.arange(NZ), np.arange(4), indexing="ij")
    freq = (4 * (NYC * z + yc) + mm).reshape(-1)
    angle = turn / 512 * ((freq[:, None] * np.arange(512)[None, :]) % 512)
    column = np.concatenate([np.cos(angle), np.sin(angle)], axis=1)
    slab_angle = turn / 128 * ((np.arange(128)[:, None] * np.arange(128)[None, :]) % 128)
    slab = np.concatenate([np.cos(slab_angle), np.sin(slab_angle)], axis=0)
    small = turn / 32 * ((np.arange(32)[:, None] * np.arange(32)[None, :]) % 32)
    cos, sin = np.cos(small), np.sin(small)
    forward = np.kron(np.eye(2), np.block([[cos, -sin], [sin, cos]]))
    backward = np.kron(np.eye(2), np.block([[cos, sin], [-sin, cos]]))
    lane = np.arange(128)
    twist = turn / LONG * (np.arange(128)[:, None] * (lane % 32)[None, :])
    sign = np.where(lane % 64 < 32, 1.0, -1.0)
    twists = np.stack([np.cos(twist), np.sin(twist) * sign]).astype(np.float32)
    classes = np.zeros((N_COL, 4, LONG), np.float32)
    for col in range(N_COL):
        for place, k in enumerate((col, 8 - col if col else 4)):
            theta = turn / LONG * ((np.arange(LONG) * k) % LONG)
            classes[col, 2 * place] = np.cos(theta)
            classes[col, 2 * place + 1] = np.sin(theta)
    taps = blur_taps()
    rows_band = np.zeros((ROWS, ROWS + 2 * HALO), jnp.bfloat16)
    for r in range(ROWS):
        rows_band[r, r : r + 2 * HALO + 1] = taps
    cols_band = np.zeros((384, 128), jnp.bfloat16)
    for c in range(128):
        cols_band[c + 64 : c + 64 + 2 * HALO + 1, c] = taps
    row_twice = (np.arange(ROWS)[:, None] // 2 == np.arange(32)[None, :]).astype(jnp.bfloat16)
    col_twice = (np.arange(128)[:, None] == np.arange(256)[None, :] // 2).astype(jnp.bfloat16)
    place = np.arange(512)
    regroup = np.zeros((512, 512), jnp.bfloat16)
    regroup[place, (place % 16) * 32 + place // 16] = 1
    return dict(
        column=np.stack(halves(column)),
        slab=np.stack(halves(slab)),
        small=np.stack(halves(forward) + halves(backward)),
        twists=twists,
        classes=classes,
        rows_band=rows_band,
        cols_band=cols_band,
        row_twice=row_twice,
        col_twice=col_twice,
        regroup=regroup,
        regroup_back=np.ascontiguousarray(regroup.T),
    )


NAMES = (
    "column",
    "slab",
    "small",
    "twists",
    "classes",
    "rows_band",
    "cols_band",
    "row_twice",
    "col_twice",
    "regroup",
    "regroup_back",
)


def mm(a, b, dims=((1,), (0,))):
    return lax.dot_general(a, b, (dims, ((), ())), preferred_element_type=F32)


def split(x):
    high = x.astype(BF16)
    return high, (x - high.astype(F32)).astype(BF16)


def swap_parts(x):
    lane = lax.broadcasted_iota(jnp.int32, x.shape, x.ndim - 1)
    return jnp.where(
        lane % 64 < 32,
        pltpu.roll(x, 96, x.ndim - 1),
        pltpu.roll(x, 32, x.ndim - 1),
    )


def kernel(
    pack_ref,
    transfer_ref,
    column_ref,
    slab_ref,
    small_ref,
    twists_ref,
    classes_ref,
    rows_band_ref,
    cols_band_ref,
    row_twice_ref,
    col_twice_ref,
    regroup_ref,
    regroup_back_ref,
    dosage_ref,
    exposure_ref,
    shots,
    doses,
    dose_out,
    spill,
    spill_out,
    t_rows,
    filt,
    cover,
    cover_side,
    cover_pool,
    weights,
    weights_side,
    extended,
    across,
    short,
    exposure_bf,
    coarse,
    uv,
    send1,
    recv1,
    send2,
    recv2,
    back2_out,
    back2,
    back1_out,
    back1,
    field_out,
    field,
    shot_send,
    shot_recv,
    dose_send,
    dose_recv,
    t_send,
    t_recv,
    y_send,
    y_recv,
    z_send,
    z_recv,
    x_send,
    x_recv,
    spill_sems,
):
    s = lax.axis_index("slab")
    c = lax.axis_index("col")
    z = s // NYC
    yc = s % NYC

    def near(offset, col):
        return (lax.rem(s + offset + N_SLAB, N_SLAB), col)

    def remote(src, dst, send_sem, recv_sem, device):
        return pltpu.make_async_remote_copy(
            src_ref=src,
            dst_ref=dst,
            send_sem=send_sem,
            recv_sem=recv_sem,
            device_id=device,
            device_id_type=MESH,
        )

    barrier = pltpu.get_barrier_semaphore()
    for offset in range(-2, 3):
        for step in range(N_COL):
            if offset or step:
                pl.semaphore_signal(
                    barrier,
                    inc=1,
                    device_id=near(offset, lax.rem(c + step, N_COL)),
                    device_id_type=MESH,
                )

    def greet_y(step, carry):
        there = z * NYC + lax.rem(yc + step, NYC)
        pl.semaphore_signal(barrier, inc=1, device_id=(there, c), device_id_type=MESH)
        return carry

    def greet_z(step, carry):
        there = lax.rem(z + step, NZ) * NYC + yc
        pl.semaphore_signal(barrier, inc=1, device_id=(there, c), device_id_type=MESH)
        return carry

    lax.fori_loop(1, NYC, greet_y, 0)
    lax.fori_loop(1, NZ, greet_z, 0)
    pl.semaphore_wait(barrier, 19 + NYC - 1 + NZ - 1)

    def to_near(source, target, sends, recvs):
        out = []
        for d in range(4):
            for step in range(N_COL):
                if d != 2 or step:
                    out.append(
                        remote(
                            source,
                            target.at[4 * d + c],
                            sends.at[4 * d + step],
                            recvs.at[4 * d + c],
                            near(2 - d, lax.rem(c + step, N_COL)),
                        )
                    )
        return out

    def from_near(source, target, sends, recvs):
        for d in range(4):
            for step in range(N_COL):
                if d != 2 or step:
                    slot = 4 * d + lax.rem(c + step, N_COL)
                    remote(
                        source, target.at[slot], sends.at[0], recvs.at[slot], (s, c)
                    ).wait_recv()

    shot_copies = to_near(pack_ref, shots, shot_send, shot_recv)
    for copy in shot_copies:
        copy.start()

    def class_row(col, place):
        return col if place == 0 else 4 + lax.rem(4 - col, 4)

    t_copies = []
    for step in range(1, N_COL):
        col = lax.rem(c + step, N_COL)
        for place in range(2):
            t_copies.append(
                remote(
                    transfer_ref.at[class_row(col, place)],
                    t_rows.at[2 * c + place],
                    t_send.at[2 * step + place],
                    t_recv.at[2 * c + place],
                    (s, col),
                )
            )
    for copy in t_copies:
        copy.start()
    for place in range(2):
        t_rows[2 * c + place] = transfer_ref[class_row(c, place)]
    shots[8 + c] = pack_ref[...]
    from_near(pack_ref, shots, shot_send, shot_recv)

    def pool_cover(col, carry):
        for d in (1, 2):
            box = jnp.transpose(shots[4 * d + col])
            start = jnp.broadcast_to(box[:, 2:3], (SLOTS, 128))
            end = jnp.broadcast_to(box[:, 3:4], (SLOTS, 128))

            def one(block, inner):
                lane = lax.broadcasted_iota(jnp.int32, (SLOTS, 128), 1) + block * 128
                left = (2 * lane + col * COLS).astype(F32)
                part = jnp.minimum(end, left + 2.0) - jnp.maximum(start, left)
                at = pl.multiple_of(block * 128, 128)
                cover_pool[col, (d - 1) * SLOTS : d * SLOTS, pl.ds(at, 128)] = jnp.maximum(
                    part, 0.0
                ).astype(BF16)
                return inner

            lax.fori_loop(0, 8, one, 0)
        return carry

    lax.fori_loop(0, N_COL, pool_cover, 0)

    def full_covers():
        for d in range(4):
            box = jnp.transpose(shots[4 * d + c])
            start = jnp.broadcast_to(box[:, 2:3], (SLOTS, 128))
            end = jnp.broadcast_to(box[:, 3:4], (SLOTS, 128))
            rows = slice(d * SLOTS, (d + 1) * SLOTS)

            def one(block, inner):
                lane = lax.broadcasted_iota(jnp.int32, (SLOTS, 128), 1) + block * 128
                pos = (lane + c * COLS).astype(F32)
                inside = (pos >= start) & (pos < end)
                at = pl.multiple_of(block * 128, 128)
                cover[rows, pl.ds(at, 128)] = jnp.where(inside, 1.0, 0.0).astype(BF16)
                return inner

            lax.fori_loop(0, COLS // 128, one, 0)
            for side in range(2):
                other = lax.rem(c + (1 if side else 3), N_COL)
                box = jnp.transpose(shots[4 * d + other])
                lane = lax.broadcasted_iota(jnp.int32, (SLOTS, 128), 1)
                pos = (lane + c * COLS + (COLS if side else -128)).astype(F32)
                inside = (pos >= box[:, 2:3]) & (pos < box[:, 3:4])
                cover_side[side, rows, :] = jnp.where(inside, 1.0, 0.0).astype(BF16)

    def make_filter():
        for step in range(1, N_COL):
            for place in range(2):
                slot = 2 * lax.rem(c + step, N_COL) + place
                remote(
                    transfer_ref.at[0], t_rows.at[slot], t_send.at[0], t_recv.at[slot], (s, c)
                ).wait_recv()
        for line in range(4):
            first, second = t_rows[2 * line], t_rows[2 * line + 1]
            stack = jnp.concatenate([first, first, second, second], axis=0)
            filt[line] = jnp.transpose(stack) * (1.0 / (LONG * LONG))

    box_own = pack_ref[...]
    dose = box_own[4:5]
    live = dose > 0.0
    area = (box_own[1:2] - box_own[0:1]) * (box_own[3:4] - box_own[2:3])
    lane_in = lax.broadcasted_iota(jnp.int32, (128, 512), 1)

    for iteration in range(ITERS):

        def dose_of(slot):
            if iteration == 0:
                value = shots[slot, 4:5, :]
            else:
                value = doses[slot]
            return value.astype(BF16).astype(F32)

        for col in range(N_COL):
            parts = []
            for d in (1, 2):
                slot = 4 * d + col
                top = 2 * lax.broadcasted_iota(jnp.int32, (32, SLOTS), 0) + s * ROWS
                top = top.astype(F32)
                part = jnp.minimum(shots[slot, 1:2, :], top + 2.0) - jnp.maximum(
                    shots[slot, 0:1, :], top
                )
                parts.append(jnp.maximum(part, 0.0) * (dose_of(slot) * 0.25))
            row_part = jnp.concatenate(parts, axis=1).astype(BF16)
            coarse[:, col * 1024 : (col + 1) * 1024] = mm(row_part, cover_pool[col])

        class_table = classes_ref[c]
        for place in range(2):
            real = jnp.zeros((32, 512), F32)
            imag = jnp.zeros((32, 512), F32)
            for q in range(8):
                block = slice(q * 512, (q + 1) * 512)
                x = coarse[:, block]
                real = real + x * class_table[2 * place : 2 * place + 1, block]
                imag = imag - x * class_table[2 * place + 1 : 2 * place + 2, block]
            at = place * 64
            for start, value in ((0, real), (32, imag)):
                high, low = split(value)
                uv[at + start : at + start + 32, 0:512] = high
                uv[128 + at + start : 128 + at + start + 32, 0:512] = low
            for start, value in ((0, imag), (32, -real)):
                high, low = split(value)
                uv[at + start : at + start + 32, 512:1024] = high
                uv[128 + at + start : 128 + at + start + 32, 512:1024] = low
        both = mm(column_ref[0], uv[...], ((1,), (1,)))
        spectrum = (
            both[:, :128] + both[:, 128:] + mm(column_ref[1], uv[0:128, :], ((1,), (1,)))
        )
        send1[iteration] = spectrum.astype(BF16).reshape(NYC, 32, 128)

        def y_copy(step, source, target):
            there = lax.rem(yc + step, NYC)
            return remote(
                source.at[iteration, there],
                target.at[iteration, yc],
                y_send.at[step],
                y_recv.at[(1 if target is back1 else 0) * ITERS + iteration, yc],
                (z * NYC + there, c),
            )

        def z_copy(step, source, target):
            there = lax.rem(z + step, NZ)
            return remote(
                source.at[iteration, there],
                target.at[iteration, z],
                z_send.at[step],
                z_recv.at[(1 if target is back2 else 0) * ITERS + iteration, z],
                (there * NYC + yc, c),
            )

        def begin(count, make, source, target, own):
            def go(step, carry):
                make(step, source, target).start()
                return carry

            lax.fori_loop(1, count, go, 0)
            target[iteration, own] = source[iteration, own]

        def finish(count, make, source, target, own, recvs, which):
            def go(step, carry):
                make(step, source, target).wait_send()
                slot = lax.rem(own + step, count)
                remote(
                    source.at[iteration, slot],
                    target.at[iteration, slot],
                    recvs.at[0, 0],
                    recvs.at[which * ITERS + iteration, slot],
                    (s, c),
                ).wait_recv()
                return carry

            lax.fori_loop(1, count, go, 0)

        begin(NYC, y_copy, send1, recv1, yc)

        if iteration == 0:
            full_covers()
        row_pos = (
            lax.broadcasted_iota(jnp.int32, (3 * ROWS, SLOTS), 0) + (s * ROWS - ROWS)
        ).astype(F32)
        for d in range(4):
            lanes = slice(d * SLOTS, (d + 1) * SLOTS)
            for place, step in enumerate((0, 3, 1)):
                slot = 4 * d + lax.rem(c + step, N_COL)
                inside = (row_pos >= shots[slot, 0:1, :]) & (row_pos < shots[slot, 1:2, :])
                value = jnp.where(inside, dose_of(slot), 0.0).astype(BF16)
                if place:
                    weights_side[place - 1, :, lanes] = value
                else:
                    weights[:, lanes] = value
        for side in range(2):
            at = side * (COLS + 128)
            block = mm(weights_side[side], cover_side[side]).astype(BF16)
            extended[:, at : at + 128] = block
            across[:, at : at + 128] = mm(rows_band_ref[...], block).astype(BF16)

        def raster(block, carry):
            at = pl.multiple_of(block * 256, 256)
            tile = mm(weights[...], cover[:, pl.ds(at, 256)]).astype(BF16)
            across[:, pl.ds(at + 128, 256)] = mm(rows_band_ref[...], tile).astype(BF16)
            return carry

        lax.fori_loop(0, COLS // 256, raster, 0)

        finish(NYC, y_copy, send1, recv1, yc, y_recv, 0)
        moved = mm(regroup_ref[...], recv1[iteration].reshape(512, 128)).astype(BF16)
        send2[iteration] = moved.reshape(NZ, 64, 128)
        begin(NZ, z_copy, send2, recv2, z)

        def blur(block, carry):
            at = pl.multiple_of(block * 128, 128)
            short[:, pl.ds(at, 128)] = mm(across[:, pl.ds(at, 384)], cols_band_ref[...])
            return carry

        lax.fori_loop(0, COLS // 128, blur, 0)
        if iteration == 0:
            make_filter()

        finish(NZ, z_copy, send2, recv2, z, z_recv, 0)

        lines = jnp.concatenate(
            [
                recv2[iteration, :, line * 16 : (line + 1) * 16, :].reshape(128, 128)
                for line in range(4)
            ],
            axis=1,
        )
        both = mm(slab_ref[0], lines) + mm(slab_ref[1], lines)
        cos_twist, sin_twist = twists_ref[0], twists_ref[1]
        sign = jnp.where(lax.broadcasted_iota(jnp.int32, (128, 128), 1) % 64 < 32, 1.0, -1.0)
        turned = []
        for line in range(4):
            lanes = slice(line * 128, (line + 1) * 128)
            value = both[:128, lanes] + sign * swap_parts(both[128:, lanes])
            turned.append(value * cos_twist + swap_parts(value) * sin_twist)
        value = jnp.concatenate(turned, axis=0)
        high, low = split(value)
        value = mm(high, small_ref[0]) + mm(low, small_ref[0]) + mm(high, small_ref[1])
        value = value * filt[...].reshape(512, 128)
        high, low = split(value)
        value = mm(high, small_ref[2]) + mm(low, small_ref[2]) + mm(high, small_ref[3])
        turned = []
        for line in range(4):
            part = value[line * 128 : (line + 1) * 128]
            turned.append(part * cos_twist - swap_parts(part) * sin_twist)
        value = jnp.concatenate(turned, axis=1)
        high, low = split(value)
        both = mm(slab_ref[0], high) + mm(slab_ref[0], low) + mm(slab_ref[1], high)
        for line in range(4):
            lanes = slice(line * 128, (line + 1) * 128)
            part = both[:128, lanes] - sign * swap_parts(both[128:, lanes])
            back2_out[iteration, :, line * 16 : (line + 1) * 16, :] = part.astype(BF16).reshape(
                NZ, 16, 128
            )
        begin(NZ, z_copy, back2_out, back2, z)
        finish(NZ, z_copy, back2_out, back2, z, z_recv, 1)
        moved = mm(regroup_back_ref[...], back2[iteration].reshape(512, 128)).astype(BF16)
        back1_out[iteration] = moved.reshape(NYC, 32, 128)
        begin(NYC, y_copy, back1_out, back1, yc)
        finish(NYC, y_copy, back1_out, back1, yc, y_recv, 1)

        held = back1[iteration].reshape(512, 128)
        both = mm(held, column_ref[0], ((0,), (0,))) + mm(held, column_ref[1], ((0,), (0,)))
        points = []
        for place in range(2):
            re = slice(place * 64, place * 64 + 32)
            im = slice(place * 64 + 32, place * 64 + 64)
            points.append(
                (both[re, :512] - both[im, 512:], both[re, 512:] + both[im, :512])
            )
        for q in range(8):
            block = slice(q * 512, (q + 1) * 512)
            total = jnp.zeros((32, 512), F32)
            for place in range(2):
                total = total + (
                    points[place][0] * class_table[2 * place : 2 * place + 1, block]
                    - points[place][1] * class_table[2 * place + 1 : 2 * place + 2, block]
                )
            at = (q % 2) * 512
            field_out[iteration, q // 2, :, at : at + 512] = total.astype(BF16)
        x_copies = []
        for step in range(1, N_COL):
            col = lax.rem(c + step, N_COL)
            x_copies.append(
                remote(
                    field_out.at[iteration, col],
                    field.at[iteration, c],
                    x_send.at[step],
                    x_recv.at[iteration, c],
                    (s, col),
                )
            )
        for copy in x_copies:
            copy.start()
        back = field_out[iteration, c].astype(F32)
        for step in range(1, N_COL):
            slot = lax.rem(c + step, N_COL)
            remote(
                field_out.at[iteration, slot],
                field.at[iteration, slot],
                x_send.at[0],
                x_recv.at[iteration, slot],
                (s, c),
            ).wait_recv()
            back = back + field[iteration, slot].astype(F32)
        for copy in x_copies:
            copy.wait_send()

        high, low = split(back)
        high = mm(row_twice_ref[...], high).astype(BF16)
        low = mm(row_twice_ref[...], low).astype(BF16)
        for block in range(8):
            lanes = slice(block * 128, (block + 1) * 128)
            wide = slice(block * 256, (block + 1) * 256)
            value = (
                short[:, wide]
                + mm(high[:, lanes], col_twice_ref[...])
                + mm(low[:, lanes], col_twice_ref[...])
            )
            if iteration == ITERS - 1:
                exposure_ref[:, wide] = value
            exposure_bf[:, wide] = value.astype(BF16)

        sums = mm(exposure_bf[...], cover[SLOTS : 3 * SLOTS, :], ((1,), (1,)))
        row_pos = (lax.broadcasted_iota(jnp.int32, (ROWS, SLOTS), 0) + s * ROWS).astype(F32)
        found = []
        for d in (1, 2):
            slot = 4 * d + c
            inside = (row_pos >= shots[slot, 0:1, :]) & (row_pos < shots[slot, 1:2, :])
            part = jnp.where(inside, sums[:, (d - 1) * SLOTS : d * SLOTS], 0.0)
            found.append(jnp.sum(part, axis=0, keepdims=True))
        spill_out[iteration] = found[0]
        copy = remote(
            spill_out.at[iteration],
            spill.at[iteration],
            spill_sems.at[0, iteration],
            spill_sems.at[1, iteration],
            near(-1, c),
        )
        copy.start()
        copy.wait()
        average = (found[1] + spill[iteration]) / area
        dose = jnp.where(live, dose * jnp.exp(RELAX * (TARGET_LEVEL - average)), 0.0)
        if iteration == 0:
            dose_out[...] = dose
            dose_copies = to_near(dose_out, doses, dose_send, dose_recv)
            for copy in dose_copies:
                copy.start()
            doses[8 + c] = dose
            from_near(dose_out, doses, dose_send, dose_recv)
            for copy in dose_copies + shot_copies + t_copies:
                copy.wait_send()
    dosage_ref[...] = dose


def per_device(shot_boxes, shot_counts, shot_doses, transfer):
    live = jnp.arange(SLOTS, dtype=jnp.int32) < shot_counts[0, 0]
    dosage = jnp.where(live, shot_doses, 0.0)
    pack = jnp.concatenate(
        [shot_boxes.astype(F32), jnp.broadcast_to(dosage[None], (4, SLOTS))], axis=0
    )
    t = tables()
    constants = [jnp.asarray(t[name]) for name in NAMES]
    vmem = pl.BlockSpec(memory_space=pltpu.VMEM)
    dma = pltpu.SemaphoreType.DMA
    dosage, exposure = pl.pallas_call(
        kernel,
        out_shape=(
            jax.ShapeDtypeStruct((1, SLOTS), F32),
            jax.ShapeDtypeStruct((ROWS, COLS), F32),
        ),
        in_specs=[vmem] * (2 + len(constants)),
        out_specs=(vmem, vmem),
        scratch_shapes=[
            pltpu.VMEM((16, 8, SLOTS), F32),
            pltpu.VMEM((16, 1, SLOTS), F32),
            pltpu.VMEM((1, SLOTS), F32),
            pltpu.VMEM((ITERS, 1, SLOTS), F32),
            pltpu.VMEM((ITERS, 1, SLOTS), F32),
            pltpu.VMEM((8, 32, 128), F32),
            pltpu.VMEM((4, 128, 128), F32),
            pltpu.VMEM((4 * SLOTS, COLS), BF16),
            pltpu.VMEM((2, 4 * SLOTS, 128), BF16),
            pltpu.VMEM((N_COL, 2 * SLOTS, 1024), BF16),
            pltpu.VMEM((3 * ROWS, 4 * SLOTS), BF16),
            pltpu.VMEM((2, 3 * ROWS, 4 * SLOTS), BF16),
            pltpu.VMEM((3 * ROWS, COLS + 256), BF16),
            pltpu.VMEM((ROWS, COLS + 256), BF16),
            pltpu.VMEM((ROWS, COLS), F32),
            pltpu.VMEM((ROWS, COLS), BF16),
            pltpu.VMEM((32, LONG), F32),
            pltpu.VMEM((256, 1024), BF16),
            pltpu.VMEM((ITERS, NYC, 32, 128), BF16),
            pltpu.VMEM((ITERS, NYC, 32, 128), BF16),
            pltpu.VMEM((ITERS, NZ, 64, 128), BF16),
            pltpu.VMEM((ITERS, NZ, 64, 128), BF16),
            pltpu.VMEM((ITERS, NZ, 64, 128), BF16),
            pltpu.VMEM((ITERS, NZ, 64, 128), BF16),
            pltpu.VMEM((ITERS, NYC, 32, 128), BF16),
            pltpu.VMEM((ITERS, NYC, 32, 128), BF16),
            pltpu.VMEM((ITERS, N_COL, 32, 1024), BF16),
            pltpu.VMEM((ITERS, N_COL, 32, 1024), BF16),
            dma((16,)),
            dma((16,)),
            dma((16,)),
            dma((16,)),
            dma((8,)),
            dma((8,)),
            dma((NYC,)),
            dma((2 * ITERS, NYC)),
            dma((NZ,)),
            dma((2 * ITERS, NZ)),
            dma((N_COL,)),
            dma((ITERS, N_COL)),
            dma((2, ITERS)),
        ],
        compiler_params=pltpu.CompilerParams(
            collective_id=0, has_side_effects=True, vmem_limit_bytes=48 << 20
        ),
        name="dose_correction",
    )(pack, transfer.reshape(8, 32, 128), *constants)
    return dosage.reshape(SLOTS), exposure


def solution(mesh):
    placed = (
        P(None, ("slab", "col")),
        P("slab", "col"),
        P(("slab", "col")),
        P(("slab", "col"), None),
    )
    return jax.shard_map(
        per_device,
        mesh=mesh,
        in_specs=placed,
        out_specs=(P(("slab", "col")), P("slab", "col")),
        check_vma=False,
    )
```

```python
import functools
import math

import jax
import jax.numpy as jnp
import numpy as np
from jax import lax
from jax.experimental import pallas as pl
from jax.experimental.pallas import tpu as pltpu
from jax.sharding import PartitionSpec as P

HALO = 64
ITERS = 2
SLOTS = 256
ROWS = 64
COLS = 2048
LONG = 4096
N_SLAB = 128
N_COL = 4
RELAX = 0.5
TARGET_LEVEL = 1.0
F32 = jnp.float32
BF16 = jnp.bfloat16
MESH = pl.DeviceIdType.MESH


def halves(values):
    high = np.asarray(values, np.float32).astype(jnp.bfloat16)
    low = (np.asarray(values, np.float64) - high.astype(np.float64)).astype(jnp.bfloat16)
    return high, low


def blur_taps():
    pos = np.arange(-HALO, HALO + 1).astype(np.float32)
    spread = np.float32(HALO / 3.0)
    raw = np.exp(np.float32(-0.5) * pos * pos / (spread * spread)).astype(np.float32)
    return (raw / raw.sum(dtype=np.float32)).astype(jnp.bfloat16)


@functools.lru_cache(None)
def tables():
    turn = 2.0 * np.pi
    angle = turn / 512 * ((np.arange(256)[:, None] * np.arange(512)[None, :]) % 512)
    column = np.concatenate([np.cos(angle), np.sin(angle)], axis=1)
    slab_angle = turn / 128 * ((np.arange(128)[:, None] * np.arange(128)[None, :]) % 128)
    pair = np.eye(2)
    slab = np.concatenate([np.kron(np.cos(slab_angle), pair), np.kron(np.sin(slab_angle), pair)])
    small = turn / 32 * ((np.arange(32)[:, None] * np.arange(32)[None, :]) % 32)
    cos, sin = np.cos(small), np.sin(small)
    forward = np.kron(pair, np.block([[cos, -sin], [sin, cos]]))
    backward = np.kron(pair, np.block([[cos, sin], [-sin, cos]]))
    lane = np.arange(128)
    scale = 2.0 ** ((lane % 32) / 32.0)
    twist = turn / LONG * np.repeat(np.arange(128), 2)[:, None] * (lane % 32)[None, :]
    sign = np.where(lane % 64 < 32, 1.0, -1.0)
    twists = np.stack(
        [
            np.cos(twist) / scale,
            np.sin(twist) * sign / scale,
            np.cos(twist) * scale,
            np.sin(twist) * sign * scale,
        ]
    ).astype(np.float32)
    classes = np.zeros((N_COL, 4, LONG), np.float32)
    for col in range(N_COL):
        for place, k in enumerate((col, col + 2048) if col else (0, 4)):
            theta = turn / LONG * ((np.arange(LONG) * k) % LONG)
            classes[col, 2 * place] = np.cos(theta)
            classes[col, 2 * place + 1] = np.sin(theta)
    taps = blur_taps()
    rows_band = np.zeros((ROWS, ROWS + 2 * HALO), jnp.bfloat16)
    for r in range(ROWS):
        rows_band[r, r : r + 2 * HALO + 1] = taps
    cols_band = np.zeros((384, 128), jnp.bfloat16)
    for c in range(128):
        cols_band[c + 64 : c + 64 + 2 * HALO + 1, c] = taps
    row_twice = (np.arange(ROWS)[:, None] // 2 == np.arange(32)[None, :]).astype(jnp.bfloat16)
    col_twice = (np.arange(128)[:, None] == np.arange(256)[None, :] // 2).astype(jnp.bfloat16)
    alternate = np.zeros((16, 512), jnp.bfloat16)
    alternate[0] = 1 - 2 * (np.arange(512) % 2)
    scales = np.stack([scale, np.zeros(128)] * 4).astype(np.float32)
    return dict(
        column=np.stack(halves(column)),
        slab=np.stack(halves(slab)),
        small=np.stack(halves(forward) + halves(backward)),
        twists=twists,
        classes=classes,
        rows_band=rows_band,
        cols_band=cols_band,
        row_twice=row_twice,
        col_twice=col_twice,
        alternate=alternate,
        scales=scales,
    )


NAMES = (
    "column",
    "slab",
    "small",
    "twists",
    "classes",
    "rows_band",
    "cols_band",
    "row_twice",
    "col_twice",
    "alternate",
    "scales",
)


def mm(a, b, dims=((1,), (0,))):
    return lax.dot_general(a, b, (dims, ((), ())), preferred_element_type=F32)


def split(x):
    high = x.astype(BF16)
    return high, (x - high.astype(F32)).astype(BF16)


def swap_parts(x):
    lane = lax.broadcasted_iota(jnp.int32, x.shape, x.ndim - 1)
    return jnp.where(
        lane % 64 < 32,
        pltpu.roll(x, 96, x.ndim - 1),
        pltpu.roll(x, 32, x.ndim - 1),
    )


def kernel(
    boxes_in,
    counts_in,
    doses_in,
    transfer_ref,
    *rest,
):
    constants_in = dict(zip(NAMES, rest[: len(NAMES)]))
    rest = rest[len(NAMES) :]
    dosage_ref, exposure_ref = rest[:2]
    held_in = dict(zip(NAMES, rest[2 : 2 + len(NAMES)]))
    (
        boxes,
        counts,
        doses_own,
        pack,
        shots,
        doses,
        sums_out,
        sums,
        spill,
        t_rows,
        filt,
        mix,
        cover,
        cover_side,
        cover_pool,
        weights,
        weights_side,
        across,
        short,
        exposure_bf,
        coarse,
        uv,
        send1,
        recv1,
        send2,
        recv2,
        field_out,
        field,
        const_sems,
        in_sems,
        shot_send,
        shot_recv,
        sums_send,
        sums_recv,
        t_send,
        t_recv,
        slab_send,
        slab_recv,
        own_sems,
        x_send,
        x_recv,
        spill_sems,
    ) = rest[2 + len(NAMES) :]
    s = lax.axis_index("slab")
    c = lax.axis_index("col")

    in_copies = [
        pltpu.make_async_copy(source, target, in_sems.at[at])
        for at, (source, target) in enumerate(
            ((boxes_in, boxes), (counts_in, counts), (doses_in, doses_own))
        )
    ]
    for copy in in_copies:
        copy.start()
    const_copies = {}
    for at, name in enumerate(NAMES):
        source = constants_in[name]
        source = source.at[c] if name == "classes" else source
        const_copies[name] = pltpu.make_async_copy(source, held_in[name], const_sems.at[at])
        const_copies[name].start()

    def near(offset, col):
        return (lax.rem(s + offset + N_SLAB, N_SLAB), col)

    def remote(src, dst, send_sem, recv_sem, device):
        return pltpu.make_async_remote_copy(
            src_ref=src,
            dst_ref=dst,
            send_sem=send_sem,
            recv_sem=recv_sem,
            device_id=device,
            device_id_type=MESH,
        )

    here = 4 * s + c
    upper = s // 64

    def t_target(k):
        if k in (1, 2, 3):
            m, place, opposite, col = here % 256, upper, 0, k
        elif k in (5, 6, 7):
            m, place, opposite, col = (511 - here) % 256, 1 - upper, 1, 8 - k
        elif k == 4:
            m, place, opposite, col = here + upper * (511 - 2 * here), 1, upper, 0
        else:
            m, place, opposite, col = (here + upper * (512 - 2 * here)) % 256, 0, upper, 0
        return m // 2, col, 4 * (m % 2) + 2 * place + opposite

    def t_source(pp, place, opposite):
        p = 2 * s + pp
        if opposite:
            other = 511 - (p + 256 * place)
            zero_col = 511 - p if place else 512 - p - 256 * jnp.where(p == 0, 1, 0)
        else:
            other = p + 256 * place
            zero_col = p
        m = jnp.where(c == 0, zero_col, other)
        return m // 4, m % 4

    barrier = pltpu.get_barrier_semaphore()

    def greet(step, carry):
        pl.semaphore_signal(
            barrier,
            inc=1,
            device_id=(lax.rem(s + step, N_SLAB), c),
            device_id_type=MESH,
        )
        return carry

    lax.fori_loop(32, N_SLAB, greet, 0)
    lax.fori_loop(1, 32, greet, 0)
    for offset in range(-2, 3):
        for step in range(1, N_COL):
            pl.semaphore_signal(
                barrier,
                inc=1,
                device_id=near(offset, lax.rem(c + step, N_COL)),
                device_id_type=MESH,
            )
    for pp in range(2):
        for place in range(2):
            for opposite in range(2):
                from_slab, from_col = t_source(pp, place, opposite)
                away = 4 * from_slab + from_col != here

                @pl.when(away)
                def _(device=(from_slab, from_col)):
                    pl.semaphore_signal(barrier, inc=1, device_id=device, device_id_type=MESH)

    for copy in in_copies:
        copy.wait()
    box_own = boxes[...].astype(F32)
    slot_id = lax.broadcasted_iota(jnp.int32, (1, SLOTS), 1)
    dose = jnp.where(slot_id < counts[...], doses_own[...], 0.0)
    pack[0:4, :] = box_own
    pack[4:8, :] = jnp.broadcast_to(dose, (4, SLOTS))
    shots[8 + c] = pack[...]

    expected = 15 + N_SLAB - 1
    for k in range(8):
        to_slab, to_col, _ = t_target(k)
        expected = expected + jnp.where(4 * to_slab + to_col != here, 1, 0)
    pl.semaphore_wait(barrier, expected)

    shot_copies = []
    for d in range(4):
        for step in range(N_COL):
            if d != 2 or step:
                shot_copies.append(
                    remote(
                        pack,
                        shots.at[4 * d + c],
                        shot_send.at[4 * d + step],
                        shot_recv.at[4 * d + c],
                        near(2 - d, lax.rem(c + step, N_COL)),
                    )
                )
    for copy in shot_copies:
        copy.start()

    t_copies = []
    for k in range(8):
        to_slab, to_col, slot = t_target(k)
        away = 4 * to_slab + to_col != here
        row = transfer_ref.at[pl.ds(k, 1)]
        distant = remote(row, t_rows.at[slot], t_send.at[k], t_recv.at[slot], (to_slab, to_col))
        local = pltpu.make_async_copy(row, t_rows.at[slot], t_recv.at[slot])
        t_copies.append((away, distant))

        @pl.when(away)
        def _(copy=distant):
            copy.start()

        @pl.when(jnp.logical_not(away))
        def _(copy=local):
            copy.start()

    def await_shots(ds):
        for d in ds:
            for step in range(N_COL):
                if d != 2 or step:
                    slot = 4 * d + lax.rem(c + step, N_COL)
                    remote(
                        pack, shots.at[slot], shot_send.at[0], shot_recv.at[slot], (s, c)
                    ).wait_recv()

    await_shots((1, 2))

    def pool_cover(col, carry):
        for d in (1, 2):
            box = jnp.transpose(shots[4 * d + col])
            start = jnp.broadcast_to(box[:, 2:3], (SLOTS, 128))
            end = jnp.broadcast_to(box[:, 3:4], (SLOTS, 128))

            def one(block, inner):
                lane = lax.broadcasted_iota(jnp.int32, (SLOTS, 128), 1) + block * 128
                left = (2 * lane + col * COLS).astype(F32)
                part = jnp.minimum(end, left + 2.0) - jnp.maximum(start, left)
                at = pl.multiple_of(block * 128, 128)
                cover_pool[col, (d - 1) * SLOTS : d * SLOTS, pl.ds(at, 128)] = jnp.maximum(
                    part, 0.0
                ).astype(BF16)
                return inner

            lax.fori_loop(0, 8, one, 0)
        return carry

    lax.fori_loop(0, N_COL, pool_cover, 0)

    def full_covers():
        await_shots((0, 3))
        for d in range(4):
            box = jnp.transpose(shots[4 * d + c])
            start = jnp.broadcast_to(box[:, 2:3], (SLOTS, 128))
            end = jnp.broadcast_to(box[:, 3:4], (SLOTS, 128))
            rows = slice(d * SLOTS, (d + 1) * SLOTS)

            def one(block, inner):
                lane = lax.broadcasted_iota(jnp.int32, (SLOTS, 128), 1) + block * 128
                pos = (lane + c * COLS).astype(F32)
                inside = (pos >= start) & (pos < end)
                at = pl.multiple_of(block * 128, 128)
                cover[rows, pl.ds(at, 128)] = jnp.where(inside, 1.0, 0.0).astype(BF16)
                return inner

            lax.fori_loop(0, COLS // 128, one, 0)
            for side in range(2):
                other = lax.rem(c + (1 if side else 3), N_COL)
                box = jnp.transpose(shots[4 * d + other])
                lane = lax.broadcasted_iota(jnp.int32, (SLOTS, 128), 1)
                pos = (lane + c * COLS + (COLS if side else -128)).astype(F32)
                inside = (pos >= box[:, 2:3]) & (pos < box[:, 3:4])
                cover_side[side, rows, :] = jnp.where(inside, 1.0, 0.0).astype(BF16)

    def blocks(row):
        return jnp.concatenate([row[:, b * 128 : (b + 1) * 128] for b in range(32)], axis=0)

    def make_filter():
        for slot in range(8):
            remote(
                transfer_ref.at[pl.ds(0, 1)],
                t_rows.at[slot],
                t_send.at[0],
                t_recv.at[slot],
                (s, c),
            ).wait_recv()
        unit = 1.0 / (LONG * LONG)
        lane = lax.broadcasted_iota(jnp.int32, (128, 128), 1)
        shared = jnp.where((lane < 64) & (here == 0), 1.0, 0.0)
        for pp in range(2):
            tables_of = []
            for opposite in range(2):
                first = blocks(t_rows[4 * pp + opposite])
                second = blocks(t_rows[4 * pp + 2 + opposite])
                stack = jnp.concatenate([first, first, second, second], axis=0)
                tables_of.append(jnp.transpose(stack) * unit)
            plus, minus = tables_of
            cross = jnp.zeros((128, 128), F32)
            if pp == 0:
                mean = 0.25 * (plus + minus)
                cross = 0.25 * (plus - minus) * shared
                plus = jnp.where(shared > 0.0, mean, plus)
                minus = jnp.where(shared > 0.0, mean, minus)
            filt[0, pl.ds(pp, 128, stride=2), :] = plus
            filt[1, pl.ds(pp, 128, stride=2), :] = minus
            mix[pl.ds(pp, 128, stride=2), :] = cross

    live = dose > 0.0
    area = (box_own[1:2] - box_own[0:1]) * (box_own[3:4] - box_own[2:3])

    def exchange(source, target, iteration, which):
        lane = which * ITERS + iteration

        def go(step, carry):
            there = lax.rem(s + step, N_SLAB)
            remote(
                source.at[iteration, pl.ds(2 * there, 2)],
                target.at[iteration, pl.ds(2 * s, 2)],
                slab_send.at[lane],
                slab_recv.at[lane],
                (there, c),
            ).start()
            return carry

        lax.fori_loop(32, N_SLAB, go, 0)
        lax.fori_loop(1, 32, go, 0)
        own = pltpu.make_async_copy(
            source.at[iteration, pl.ds(2 * s, 2)],
            target.at[iteration, pl.ds(2 * s, 2)],
            own_sems.at[lane],
        )
        own.start()
        whole = remote(
            source.at[iteration, pl.ds(0, 2 * N_SLAB - 2)],
            target.at[iteration, pl.ds(0, 2 * N_SLAB - 2)],
            slab_send.at[lane],
            slab_recv.at[lane],
            (lax.rem(s + 1, N_SLAB), c),
        )
        return own, whole

    def arrived(pair):
        own, whole = pair
        own.wait()
        whole.wait_recv()

    lane_id = lax.broadcasted_iota(jnp.int32, (256, 128), 1)
    sign = jnp.where(lane_id % 64 < 32, 1.0, -1.0)
    sent = []
    ready = set()

    def const(name):
        if name not in ready:
            ready.add(name)
            const_copies[name].wait()
        return held_in[name]

    for iteration in range(ITERS):

        def dose_of(slot):
            value = shots[slot, 4:5, :] if iteration == 0 else doses[slot]
            return value.astype(BF16).astype(F32)

        for col in range(N_COL):
            parts = []
            for d in (1, 2):
                slot = 4 * d + col
                top = 2 * lax.broadcasted_iota(jnp.int32, (32, SLOTS), 0) + s * ROWS
                top = top.astype(F32)
                part = jnp.minimum(shots[slot, 1:2, :], top + 2.0) - jnp.maximum(
                    shots[slot, 0:1, :], top
                )
                parts.append(jnp.maximum(part, 0.0) * (dose_of(slot) * 0.25))
            row_part = jnp.concatenate(parts, axis=1).astype(BF16)
            coarse[:, col * 1024 : (col + 1) * 1024] = mm(row_part, cover_pool[col])

        classes = const("classes")
        for place in range(2):
            real = jnp.zeros((32, 512), F32)
            imag = jnp.zeros((32, 512), F32)
            for q in range(8):
                block = slice(q * 512, (q + 1) * 512)
                x = coarse[:, block]
                real = real + x * classes[2 * place : 2 * place + 1, block]
                imag = imag - x * classes[2 * place + 1 : 2 * place + 2, block]
            at = place * 64
            real_high, real_low = split(real)
            imag_high, imag_low = split(imag)
            for base, re, im in ((at, real_high, imag_high), (128 + at, real_low, imag_low)):
                uv[base : base + 32, 0:512] = re
                uv[base + 32 : base + 64, 0:512] = im
                uv[base : base + 32, 512:1024] = im
                uv[base + 32 : base + 64, 512:1024] = -re
        column = const("column")
        both = mm(column[0], uv[...], ((1,), (1,)))
        spectrum = both[:, :128] + both[:, 128:] + mm(column[1], uv[0:128, :], ((1,), (1,)))
        alternate = const("alternate")
        both = mm(alternate[...], uv[:, 512:1024], ((1,), (1,)))
        nyquist = both[:, :128] + both[:, 128:]
        lane16 = lax.broadcasted_iota(jnp.int32, (16, 128), 1)
        chosen = (lane16 >= 32) & (lane16 < 64) & (c == 0)
        nyquist = jnp.where(chosen, nyquist, 0.0)
        scales = const("scales")
        scale = scales[0:1, :]
        send1[iteration] = (spectrum * scale).astype(BF16)
        send1[iteration, 0:16, :] = ((spectrum[0:16] - nyquist) * scale).astype(BF16)
        moving = exchange(send1, recv1, iteration, 0)
        sent.append(moving[1])

        if iteration == 0:
            full_covers()
        row_pos = (
            lax.broadcasted_iota(jnp.int32, (3 * ROWS, SLOTS), 0) + (s * ROWS - ROWS)
        ).astype(F32)
        for d in range(4):
            lanes = slice(d * SLOTS, (d + 1) * SLOTS)
            for place, step in enumerate((0, 3, 1)):
                slot = 4 * d + lax.rem(c + step, N_COL)
                inside = (row_pos >= shots[slot, 0:1, :]) & (row_pos < shots[slot, 1:2, :])
                value = jnp.where(inside, dose_of(slot), 0.0).astype(BF16)
                if place:
                    weights_side[place - 1, :, lanes] = value
                else:
                    weights[:, lanes] = value
        rows_band = const("rows_band")
        cols_band = const("cols_band")
        for side in range(2):
            at = side * (COLS + 128)
            block = mm(weights_side[side], cover_side[side]).astype(BF16)
            across[:, at : at + 128] = mm(rows_band[...], block).astype(BF16)

        def raster(block, carry):
            at = pl.multiple_of(block * 256, 256)
            tile = mm(weights[...], cover[:, pl.ds(at, 256)]).astype(BF16)
            across[:, pl.ds(at + 128, 256)] = mm(rows_band[...], tile).astype(BF16)
            return carry

        lax.fori_loop(0, COLS // 256, raster, 0)

        def blur(block, carry):
            at = pl.multiple_of(block * 128, 128)
            short[:, pl.ds(at, 128)] = mm(across[:, pl.ds(at, 384)], cols_band[...])
            return carry

        lax.fori_loop(0, COLS // 128, blur, 0)
        if iteration == 0:
            make_filter()
        slab = const("slab")
        small = const("small")
        twists = const("twists")

        arrived(moving)
        lines = recv1[iteration]
        both = mm(slab[0], lines) + mm(slab[1], lines)
        part = sign * both[:256]
        other = swap_parts(both[256:])
        turned = []
        for value in (sign * (part + other), part - other):
            turned.append(value * twists[0] + swap_parts(value) * twists[1])
        high, low = split(jnp.concatenate(turned, axis=0))
        value = mm(high, small[0]) + mm(low, small[0]) + mm(high, small[1])
        line, mirror = value[:256], value[256:]
        cross = mix[...]
        value = jnp.concatenate(
            [line * filt[0] + mirror * cross, mirror * filt[1] + line * cross], axis=0
        )
        high, low = split(value)
        value = mm(high, small[2]) + mm(low, small[2]) + mm(high, small[3])
        turned = []
        for part in (value[:256], value[256:]):
            turned.append(part * twists[2] - swap_parts(part) * twists[3])
        line, mirror = turned[0], sign * turned[1]
        high, low = split(line + mirror)
        both = mm(slab[0, 0:256], jnp.concatenate([high, low], axis=1))
        real_part = both[:, :128] + both[:, 128:] + mm(slab[1, 0:256], high)
        high, low = split(line - mirror)
        both = mm(slab[0, 256:512], jnp.concatenate([high, low], axis=1))
        imag_part = both[:, :128] + both[:, 128:] + mm(slab[1, 256:512], high)
        send2[iteration] = (real_part - sign * swap_parts(imag_part)).astype(BF16)
        moving = exchange(send2, recv2, iteration, 1)
        sent.append(moving[1])
        row_twice = const("row_twice")
        col_twice = const("col_twice")
        arrived(moving)

        held = recv2[iteration]
        both = mm(held, column[0], ((0,), (0,))) + mm(held, column[1], ((0,), (0,)))
        nyquist = mm(held[0:16], alternate[...], ((0,), (0,)))[32:64]
        points = []
        for place in range(2):
            re = slice(place * 64, place * 64 + 32)
            im = slice(place * 64 + 32, place * 64 + 64)
            points.append(
                (both[re, :512] - both[im, 512:], both[re, 512:] + both[im, :512])
            )
        points[0] = (points[0][0] + jnp.where(c == 0, nyquist, 0.0), points[0][1])

        x_copies = []
        for step in (2, 1, 3, 0):
            quarter = lax.rem(c + step, N_COL)
            for half in range(2):
                at = pl.multiple_of(quarter * 1024 + half * 512, 512)
                total = jnp.zeros((32, 512), F32)
                for place in range(2):
                    total = total + (
                        points[place][0] * classes[2 * place : 2 * place + 1, pl.ds(at, 512)]
                        - points[place][1]
                        * classes[2 * place + 1 : 2 * place + 2, pl.ds(at, 512)]
                    )
                field_out[iteration, step, :, half * 512 : (half + 1) * 512] = total.astype(BF16)
            if step:
                copy = remote(
                    field_out.at[iteration, step],
                    field.at[iteration, step],
                    x_send.at[iteration, step],
                    x_recv.at[iteration, step],
                    (s, quarter),
                )
                copy.start()
                x_copies.append(copy)
        back = field_out[iteration, 0].astype(F32)
        for step, copy in zip((2, 1, 3), x_copies):
            copy.wait_recv()
            back = back + field[iteration, step].astype(F32)
        row = lax.broadcasted_iota(jnp.int32, (32, 1024), 0).astype(F32)
        back = back * jnp.exp(row * (-math.log(2.0) / 32.0))

        high, low = split(back)
        high = mm(row_twice[...], high).astype(BF16)
        low = mm(row_twice[...], low).astype(BF16)
        for block in range(8):
            lanes = slice(block * 128, (block + 1) * 128)
            wide = slice(block * 256, (block + 1) * 256)
            value = (
                short[:, wide] + mm(high[:, lanes], col_twice[...]) + mm(low[:, lanes], col_twice[...])
            )
            if iteration == ITERS - 1:
                exposure_ref[:, wide] = value
            exposure_bf[:, wide] = value.astype(BF16)

        measured = mm(exposure_bf[...], cover[SLOTS : 3 * SLOTS, :], ((1,), (1,)))
        row_pos = (lax.broadcasted_iota(jnp.int32, (ROWS, SLOTS), 0) + s * ROWS).astype(F32)
        for d in (1, 2):
            slot = 4 * d + c
            inside = (row_pos >= shots[slot, 0:1, :]) & (row_pos < shots[slot, 1:2, :])
            part = jnp.where(inside, measured[:, (d - 1) * SLOTS : d * SLOTS], 0.0)
            sums_out[iteration, d - 1 : d, :] = jnp.sum(part, axis=0, keepdims=True)
        sent.extend(x_copies)
        if iteration == 0:
            for offset in (2, -2, 1, -1, 0):
                for step in range(N_COL):
                    if offset or step:
                        copy = remote(
                            sums_out.at[iteration],
                            sums.at[4 * (2 - offset) + c],
                            sums_send.at[4 * (2 - offset) + step],
                            sums_recv.at[4 * (2 - offset) + c],
                            near(offset, lax.rem(c + step, N_COL)),
                        )
                        copy.start()
                        sent.append(copy)
            sums[8 + c] = sums_out[iteration]
            for place in range(5):
                for step in range(N_COL):
                    if place != 2 or step:
                        slot = 4 * place + lax.rem(c + step, N_COL)
                        remote(
                            sums_out.at[iteration],
                            sums.at[slot],
                            sums_send.at[0],
                            sums_recv.at[slot],
                            (s, c),
                        ).wait_recv()
            for slot in range(4 * N_COL):
                box = shots[slot]
                whole_area = (box[1:2] - box[0:1]) * (box[3:4] - box[2:3])
                average = (sums[slot, 1:2, :] + sums[slot + N_COL, 0:1, :]) / whole_area
                past = box[4:5]
                doses[slot] = jnp.where(
                    past > 0.0, past * jnp.exp(RELAX * (TARGET_LEVEL - average)), 0.0
                )
        else:
            copy = remote(
                sums_out.at[iteration],
                spill,
                spill_sems.at[0],
                spill_sems.at[1],
                near(-1, c),
            )
            copy.start()
            for other in sent:
                other.wait_send()
            for other in shot_copies:
                other.wait_send()
            for away, other in t_copies:

                @pl.when(away)
                def _(other=other):
                    other.wait_send()

            copy.wait()
            average = (sums_out[iteration, 1:2, :] + spill[0:1, :]) / area
            dose = doses[8 + c]
            dosage_ref[...] = jnp.where(
                live, dose * jnp.exp(RELAX * (TARGET_LEVEL - average)), 0.0
            )


def per_device(shot_boxes, shot_counts, shot_doses, transfer):
    t = tables()
    constants = [jnp.asarray(t[name]) for name in NAMES]
    vmem = pl.BlockSpec(memory_space=pltpu.VMEM)
    stay = pl.BlockSpec(memory_space=pl.ANY)
    dma = pltpu.SemaphoreType.DMA
    held = [
        pltpu.VMEM(value.shape[1:] if name == "classes" else value.shape, value.dtype)
        for name, value in zip(NAMES, constants)
    ]
    dosage, exposure = pl.pallas_call(
        kernel,
        out_shape=(
            jax.ShapeDtypeStruct((1, SLOTS), F32),
            jax.ShapeDtypeStruct((ROWS, COLS), F32),
        ),
        in_specs=[stay] * (4 + len(constants)),
        out_specs=(vmem, vmem),
        scratch_shapes=[
            *held,
            pltpu.VMEM((4, SLOTS), jnp.int32),
            pltpu.VMEM((1, 1), jnp.int32),
            pltpu.VMEM((1, SLOTS), F32),
            pltpu.VMEM((8, SLOTS), F32),
            pltpu.VMEM((16, 8, SLOTS), F32),
            pltpu.VMEM((16, 1, SLOTS), F32),
            pltpu.VMEM((ITERS, 2, SLOTS), F32),
            pltpu.VMEM((20, 2, SLOTS), F32),
            pltpu.VMEM((2, SLOTS), F32),
            pltpu.VMEM((8, 1, LONG), F32),
            pltpu.VMEM((2, 256, 128), F32),
            pltpu.VMEM((256, 128), F32),
            pltpu.VMEM((4 * SLOTS, COLS), BF16),
            pltpu.VMEM((2, 4 * SLOTS, 128), BF16),
            pltpu.VMEM((N_COL, 2 * SLOTS, 1024), BF16),
            pltpu.VMEM((3 * ROWS, 4 * SLOTS), BF16),
            pltpu.VMEM((2, 3 * ROWS, 4 * SLOTS), BF16),
            pltpu.VMEM((ROWS, COLS + 256), BF16),
            pltpu.VMEM((ROWS, COLS), F32),
            pltpu.VMEM((ROWS, COLS), BF16),
            pltpu.VMEM((32, LONG), F32),
            pltpu.VMEM((256, 1024), BF16),
            pltpu.VMEM((ITERS, 2 * N_SLAB, 128), BF16),
            pltpu.VMEM((ITERS, 2 * N_SLAB, 128), BF16),
            pltpu.VMEM((ITERS, 2 * N_SLAB, 128), BF16),
            pltpu.VMEM((ITERS, 2 * N_SLAB, 128), BF16),
            pltpu.VMEM((ITERS, N_COL, 32, 1024), BF16),
            pltpu.VMEM((ITERS, N_COL, 32, 1024), BF16),
            dma((len(NAMES),)),
            dma((3,)),
            dma((16,)),
            dma((16,)),
            dma((20,)),
            dma((20,)),
            dma((8,)),
            dma((8,)),
            dma((2 * ITERS,)),
            dma((2 * ITERS,)),
            dma((2 * ITERS,)),
            dma((ITERS, N_COL)),
            dma((ITERS, N_COL)),
            dma((2,)),
        ],
        compiler_params=pltpu.CompilerParams(
            collective_id=0, has_side_effects=True, vmem_limit_bytes=60 << 20
        ),
        name="dose_correction",
    )(shot_boxes, shot_counts, shot_doses.reshape(1, SLOTS), transfer, *constants)
    return dosage.reshape(SLOTS), exposure


def solution(mesh):
    placed = (
        P(None, ("slab", "col")),
        P("slab", "col"),
        P(("slab", "col")),
        P(("slab", "col"), None),
    )
    return jax.shard_map(
        per_device,
        mesh=mesh,
        in_specs=placed,
        out_specs=(P(("slab", "col")), P("slab", "col")),
        check_vma=False,
    )
```

```python
import functools
import math

import jax
import jax.numpy as jnp
import numpy as np
from jax import lax
from jax.experimental import pallas as pl
from jax.experimental.pallas import tpu as pltpu
from jax.sharding import PartitionSpec as P

HALO = 64
ITERS = 2
SLOTS = 256
ROWS = 64
COLS = 2048
LONG = 4096
N_SLAB = 128
N_COL = 4
RELAX = 0.5
TARGET_LEVEL = 1.0
F32 = jnp.float32
BF16 = jnp.bfloat16
MESH = pl.DeviceIdType.MESH


def halves(values):
    high = np.asarray(values, np.float32).astype(jnp.bfloat16)
    low = (np.asarray(values, np.float64) - high.astype(np.float64)).astype(jnp.bfloat16)
    return high, low


def blur_taps():
    pos = np.arange(-HALO, HALO + 1).astype(np.float32)
    spread = np.float32(HALO / 3.0)
    raw = np.exp(np.float32(-0.5) * pos * pos / (spread * spread)).astype(np.float32)
    return (raw / raw.sum(dtype=np.float32)).astype(jnp.bfloat16)


@functools.lru_cache(None)
def tables():
    turn = 2.0 * np.pi
    angle = turn / 512 * ((np.arange(256)[:, None] * np.arange(512)[None, :]) % 512)
    column = np.concatenate([np.cos(angle), np.sin(angle)], axis=1)
    slab_angle = turn / 128 * ((np.arange(128)[:, None] * np.arange(128)[None, :]) % 128)
    pair = np.eye(2)
    slab = np.concatenate([np.kron(np.cos(slab_angle), pair), np.kron(np.sin(slab_angle), pair)])
    small = turn / 32 * ((np.arange(32)[:, None] * np.arange(32)[None, :]) % 32)
    cos, sin = np.cos(small), np.sin(small)
    cos, sin = np.kron(pair, cos), np.kron(pair, sin)
    forward = np.block([[cos, -sin], [sin, cos]])
    backward = np.block([[cos, sin], [-sin, cos]])
    lane = np.arange(128)
    scale = 2.0 ** ((lane % 32) / 32.0)
    twist = turn / LONG * np.repeat(np.arange(128), 2)[:, None] * (lane % 32)[None, :]
    sign = np.where(lane < 64, 1.0, -1.0)
    twists = np.stack(
        [
            np.cos(twist) / scale,
            np.sin(twist) * sign / scale,
            np.cos(twist) * scale,
            np.sin(twist) * sign * scale,
        ]
    ).astype(np.float32)
    classes = np.zeros((N_COL, 4, LONG), np.float32)
    for col in range(N_COL):
        for place, k in enumerate((col, col + 2048) if col else (0, 4)):
            theta = turn / LONG * ((np.arange(LONG) * k) % LONG)
            classes[col, 2 * place] = np.cos(theta)
            classes[col, 2 * place + 1] = np.sin(theta)
    taps = blur_taps()
    rows_band = np.zeros((ROWS, ROWS + 2 * HALO), jnp.bfloat16)
    for r in range(ROWS):
        rows_band[r, r : r + 2 * HALO + 1] = taps
    cols_band = np.zeros((384, 128), jnp.bfloat16)
    for c in range(128):
        cols_band[c + 64 : c + 64 + 2 * HALO + 1, c] = taps
    row_twice = (np.arange(ROWS)[:, None] // 2 == np.arange(32)[None, :]).astype(jnp.bfloat16)
    col_twice = (np.arange(256)[:, None] % 128 == np.arange(256)[None, :] // 2).astype(
        jnp.bfloat16
    )
    alternate = np.zeros((16, 512), jnp.bfloat16)
    alternate[0] = 1 - 2 * (np.arange(512) % 2)
    scales = np.stack([scale, np.zeros(128)] * 4).astype(np.float32)
    return dict(
        column=np.stack(halves(column)),
        slab=np.stack(halves(slab)),
        small=np.stack(halves(forward) + halves(backward)),
        twists=twists,
        classes=classes,
        rows_band=rows_band,
        cols_band=cols_band,
        row_twice=row_twice,
        col_twice=col_twice,
        alternate=alternate,
        scales=scales,
    )


NAMES = (
    "column",
    "slab",
    "small",
    "twists",
    "classes",
    "rows_band",
    "cols_band",
    "row_twice",
    "col_twice",
    "alternate",
    "scales",
)


def mm(a, b, dims=((1,), (0,))):
    return lax.dot_general(a, b, (dims, ((), ())), preferred_element_type=F32)


def split(x):
    high = x.astype(BF16)
    return high, (x - high.astype(F32)).astype(BF16)


def swap_parts(x):
    return pltpu.roll(x, 64, 1)


def over_slabs(act):
    def turn(group, carry):
        for place in range(8):
            act(group * 8 + place)
        return carry

    lax.fori_loop(6, 16, turn, 0)
    lax.fori_loop(1, 6, turn, 0)
    for step in range(1, 8):
        act(step)


def kernel(
    boxes_in,
    counts_in,
    doses_in,
    transfer_ref,
    *rest,
):
    constants_in = dict(zip(NAMES, rest[: len(NAMES)]))
    rest = rest[len(NAMES) :]
    dosage_ref, exposure_ref = rest[:2]
    held_in = dict(zip(NAMES, rest[2 : 2 + len(NAMES)]))
    (
        boxes,
        counts,
        doses_own,
        pack,
        shots,
        doses,
        sums_out,
        sums,
        spill,
        t_rows,
        filt,
        mix,
        cover,
        cover_side,
        cover_pool,
        weights,
        weights_side,
        across,
        short,
        exposure_bf,
        coarse,
        uv,
        send1,
        recv1,
        send2,
        recv2,
        field_out,
        field,
        const_sems,
        in_sems,
        shot_send,
        shot_recv,
        sums_send,
        sums_recv,
        t_send,
        t_recv,
        slab_send,
        slab_recv,
        own_sems,
        x_send,
        x_recv,
        spill_sems,
    ) = rest[2 + len(NAMES) :]
    s = lax.axis_index("slab")
    c = lax.axis_index("col")

    in_copies = [
        pltpu.make_async_copy(source, target, in_sems.at[at])
        for at, (source, target) in enumerate(
            ((boxes_in, boxes), (counts_in, counts), (doses_in, doses_own))
        )
    ]
    for copy in in_copies:
        copy.start()
    const_copies = {}
    for at, name in enumerate(NAMES):
        source = constants_in[name]
        source = source.at[c] if name == "classes" else source
        const_copies[name] = pltpu.make_async_copy(source, held_in[name], const_sems.at[at])
        const_copies[name].start()

    def near(offset, col):
        return (lax.rem(s + offset + N_SLAB, N_SLAB), col)

    def remote(src, dst, send_sem, recv_sem, device):
        return pltpu.make_async_remote_copy(
            src_ref=src,
            dst_ref=dst,
            send_sem=send_sem,
            recv_sem=recv_sem,
            device_id=device,
            device_id_type=MESH,
        )

    here = 4 * s + c
    upper = s // 64

    def t_target(k):
        if k in (1, 2, 3):
            m, place, opposite, col = here % 256, upper, 0, k
        elif k in (5, 6, 7):
            m, place, opposite, col = (511 - here) % 256, 1 - upper, 1, 8 - k
        elif k == 4:
            m, place, opposite, col = here + upper * (511 - 2 * here), 1, upper, 0
        else:
            m, place, opposite, col = (here + upper * (512 - 2 * here)) % 256, 0, upper, 0
        return m // 2, col, 4 * (m % 2) + 2 * place + opposite

    def t_source(pp, place, opposite):
        p = 2 * s + pp
        if opposite:
            other = 511 - (p + 256 * place)
            zero_col = 511 - p if place else 512 - p - 256 * jnp.where(p == 0, 1, 0)
        else:
            other = p + 256 * place
            zero_col = p
        m = jnp.where(c == 0, zero_col, other)
        return m // 4, m % 4

    barrier = pltpu.get_barrier_semaphore()

    def greet(step):
        pl.semaphore_signal(
            barrier,
            inc=1,
            device_id=(lax.rem(s + step, N_SLAB), c),
            device_id_type=MESH,
        )

    over_slabs(greet)
    for offset in range(-2, 3):
        for step in range(1, N_COL):
            pl.semaphore_signal(
                barrier,
                inc=1,
                device_id=near(offset, lax.rem(c + step, N_COL)),
                device_id_type=MESH,
            )
    for pp in range(2):
        for place in range(2):
            for opposite in range(2):
                from_slab, from_col = t_source(pp, place, opposite)
                away = 4 * from_slab + from_col != here

                @pl.when(away)
                def _(device=(from_slab, from_col)):
                    pl.semaphore_signal(barrier, inc=1, device_id=device, device_id_type=MESH)

    for copy in in_copies:
        copy.wait()
    box_own = boxes[...].astype(F32)
    slot_id = lax.broadcasted_iota(jnp.int32, (1, SLOTS), 1)
    dose = jnp.where(slot_id < counts[...], doses_own[...], 0.0)
    pack[0:4, :] = box_own
    pack[4:8, :] = jnp.broadcast_to(dose, (4, SLOTS))
    shots[8 + c] = pack[...]

    def from_block(col):
        begins, ends, firsts = [], [], []
        for d in (1, 2):
            box = shots[4 * d + col]
            begin = box[2:3] - (col * COLS).astype(F32)
            first = jnp.floor(begin * (1.0 / 256.0))
            begins.append(begin - first * 256.0 - 64.0)
            ends.append(box[3:4] - (col * COLS).astype(F32) - first * 256.0 - 64.0)
            firsts.append(first)
        return tuple(jnp.concatenate(parts, axis=1) for parts in (begins, ends, firsts))

    def pool_cover(col, carry):
        begin, end, _ = from_block(col)
        row = lax.broadcasted_iota(jnp.int32, (16, 2 * SLOTS), 0)
        both = jnp.where(row == 0, begin, jnp.where(row == 1, end, 0.0)).astype(BF16)
        row = lax.broadcasted_iota(jnp.int32, (16, 256), 0)
        lane = lax.broadcasted_iota(jnp.int32, (16, 256), 1)
        pick = jnp.where(row == lane // 128, 1.0, 0.0).astype(BF16)
        wide = mm(both, pick, ((0,), (0,)))
        begin, end = wide[:, :128], wide[:, 128:]
        for part in range(2):
            lane = lax.broadcasted_iota(jnp.int32, (2 * SLOTS, 128), 1)
            left = (2 * lane + (256 * part - 64)).astype(F32)
            inside = jnp.minimum(end, left + 2.0) - jnp.maximum(begin, left)
            cover_pool[col, :, part * 128 : (part + 1) * 128] = jnp.maximum(inside, 0.0).astype(
                BF16
            )
        return carry

    def full_covers(ds):
        for d in ds:
            box = jnp.transpose(shots[4 * d + c])
            start = jnp.broadcast_to(box[:, 2:3], (SLOTS, 128))
            end = jnp.broadcast_to(box[:, 3:4], (SLOTS, 128))
            rows = slice(d * SLOTS, (d + 1) * SLOTS)

            def one(block, inner):
                lane = lax.broadcasted_iota(jnp.int32, (SLOTS, 128), 1) + block * 128
                pos = (lane + c * COLS).astype(F32)
                inside = (pos >= start) & (pos < end)
                at = pl.multiple_of(block * 128, 128)
                cover[rows, pl.ds(at, 128)] = jnp.where(inside, 1.0, 0.0).astype(BF16)
                return inner

            lax.fori_loop(0, COLS // 128, one, 0)

    def side_covers():
        for d in range(4):
            rows = slice(d * SLOTS, (d + 1) * SLOTS)
            for side in range(2):
                other = lax.rem(c + (1 if side else 3), N_COL)
                box = jnp.transpose(shots[4 * d + other])
                lane = lax.broadcasted_iota(jnp.int32, (SLOTS, 128), 1)
                pos = (lane + c * COLS + (COLS if side else -128)).astype(F32)
                inside = (pos >= box[:, 2:3]) & (pos < box[:, 3:4])
                cover_side[side, rows, :] = jnp.where(inside, 1.0, 0.0).astype(BF16)

    full_covers((2,))

    expected = 15 + N_SLAB - 1
    for k in range(8):
        to_slab, to_col, _ = t_target(k)
        expected = expected + jnp.where(4 * to_slab + to_col != here, 1, 0)
    pl.semaphore_wait(barrier, expected)

    shot_copies = []
    for d in range(4):
        for step in range(N_COL):
            if d != 2 or step:
                shot_copies.append(
                    remote(
                        pack,
                        shots.at[4 * d + c],
                        shot_send.at[4 * d + step],
                        shot_recv.at[4 * d + c],
                        near(2 - d, lax.rem(c + step, N_COL)),
                    )
                )
    for copy in shot_copies:
        copy.start()

    t_copies = []
    for k in range(8):
        to_slab, to_col, slot = t_target(k)
        away = 4 * to_slab + to_col != here
        row = transfer_ref.at[pl.ds(k, 1)]
        distant = remote(row, t_rows.at[slot], t_send.at[k], t_recv.at[slot], (to_slab, to_col))
        local = pltpu.make_async_copy(row, t_rows.at[slot], t_recv.at[slot])
        t_copies.append((away, distant))

        @pl.when(away)
        def _(copy=distant):
            copy.start()

        @pl.when(jnp.logical_not(away))
        def _(copy=local):
            copy.start()

    def await_shots(ds):
        for d in ds:
            for step in range(N_COL):
                if d != 2 or step:
                    slot = 4 * d + lax.rem(c + step, N_COL)
                    remote(
                        pack, shots.at[slot], shot_send.at[0], shot_recv.at[slot], (s, c)
                    ).wait_recv()

    await_shots((1, 2))

    lax.fori_loop(0, N_COL, pool_cover, 0)

    def blocks(row):
        return jnp.concatenate([row[:, b * 128 : (b + 1) * 128] for b in range(32)], axis=0)

    def make_filter():
        for slot in range(8):
            remote(
                transfer_ref.at[pl.ds(0, 1)],
                t_rows.at[slot],
                t_send.at[0],
                t_recv.at[slot],
                (s, c),
            ).wait_recv()
        unit = 1.0 / (LONG * LONG)
        lane = lax.broadcasted_iota(jnp.int32, (128, 128), 1)
        shared = jnp.where((lane % 64 < 32) & (here == 0), 1.0, 0.0)
        for pp in range(2):
            tables_of = []
            for opposite in range(2):
                first = blocks(t_rows[4 * pp + opposite])
                second = blocks(t_rows[4 * pp + 2 + opposite])
                stack = jnp.concatenate([first, second, first, second], axis=0)
                tables_of.append(jnp.transpose(stack) * unit)
            plus, minus = tables_of
            cross = jnp.zeros((128, 128), F32)
            if pp == 0:
                mean = 0.25 * (plus + minus)
                cross = 0.25 * (plus - minus) * shared
                plus = jnp.where(shared > 0.0, mean, plus)
                minus = jnp.where(shared > 0.0, mean, minus)
            filt[0, pl.ds(pp, 128, stride=2), :] = plus
            filt[1, pl.ds(pp, 128, stride=2), :] = minus
            mix[pl.ds(pp, 128, stride=2), :] = cross

    live = dose > 0.0
    area = (box_own[1:2] - box_own[0:1]) * (box_own[3:4] - box_own[2:3])

    def exchange(source, target, iteration, which):
        lane = which * ITERS + iteration

        def go(step):
            there = lax.rem(s + step, N_SLAB)
            remote(
                source.at[iteration, there],
                target.at[iteration, s],
                slab_send.at[lane],
                slab_recv.at[lane],
                (there, c),
            ).start()

        over_slabs(go)
        own = pltpu.make_async_copy(
            source.at[iteration, s],
            target.at[iteration, s],
            own_sems.at[lane],
        )
        own.start()
        whole = remote(
            source.at[iteration, pl.ds(0, N_SLAB - 1)],
            target.at[iteration, pl.ds(0, N_SLAB - 1)],
            slab_send.at[lane],
            slab_recv.at[lane],
            (lax.rem(s + 1, N_SLAB), c),
        )
        return own, whole

    def arrived(pair):
        own, whole = pair
        own.wait()
        whole.wait_recv()

    lane_id = lax.broadcasted_iota(jnp.int32, (256, 128), 1)
    sign = jnp.where(lane_id < 64, 1.0, -1.0)
    sent = []
    ready = set()

    def const(name):
        if name not in ready:
            ready.add(name)
            const_copies[name].wait()
        return held_in[name]

    for iteration in range(ITERS):

        def dose_of(slot):
            value = shots[slot, 4:5, :] if iteration == 0 else doses[slot]
            return value.astype(BF16).astype(F32)

        for col in range(N_COL):
            parts = []
            for d in (1, 2):
                slot = 4 * d + col
                top = 2 * lax.broadcasted_iota(jnp.int32, (32, SLOTS), 0) + s * ROWS
                top = top.astype(F32)
                part = jnp.minimum(shots[slot, 1:2, :], top + 2.0) - jnp.maximum(
                    shots[slot, 0:1, :], top
                )
                parts.append(jnp.maximum(part, 0.0) * (dose_of(slot) * 0.25))
            row_part = jnp.concatenate(parts, axis=1)
            first = from_block(jnp.int32(col))[2]
            placed = jnp.concatenate(
                [
                    (row_part * jnp.where(first == float(b), 1.0, 0.0)).astype(BF16)
                    for b in range(8)
                ],
                axis=0,
            )
            tile = mm(placed, cover_pool[col])
            for b in range(8):
                at = col * 1024 + b * 128
                block = tile[b * 32 : (b + 1) * 32, :128]
                if b:
                    block = block + tile[(b - 1) * 32 : b * 32, 128:]
                coarse[:, at : at + 128] = block

        classes = const("classes")
        for place in range(2):
            real = jnp.zeros((32, 512), F32)
            imag = jnp.zeros((32, 512), F32)
            for q in range(8):
                block = slice(q * 512, (q + 1) * 512)
                x = coarse[:, block]
                real = real + x * classes[2 * place : 2 * place + 1, block]
                imag = imag - x * classes[2 * place + 1 : 2 * place + 2, block]
            at = place * 32
            real_high, real_low = split(real)
            imag_high, imag_low = split(imag)
            for base, re, im in ((at, real_high, imag_high), (128 + at, real_low, imag_low)):
                uv[base : base + 32, 0:512] = re
                uv[base + 64 : base + 96, 0:512] = im
                uv[base : base + 32, 512:1024] = im
                uv[base + 64 : base + 96, 512:1024] = -re
        column = const("column")
        both = mm(column[0], uv[...], ((1,), (1,)))
        spectrum = both[:, :128] + both[:, 128:] + mm(column[1], uv[0:128, :], ((1,), (1,)))
        alternate = const("alternate")
        both = mm(alternate[...], uv[:, 512:1024], ((1,), (1,)))
        nyquist = both[:, :128] + both[:, 128:]
        lane16 = lax.broadcasted_iota(jnp.int32, (16, 128), 1)
        chosen = (lane16 >= 64) & (lane16 < 96) & (c == 0)
        nyquist = jnp.where(chosen, nyquist, 0.0)
        scales = const("scales")
        scale = scales[0:1, :]
        spectrum = jnp.concatenate([spectrum[0:16] - nyquist, spectrum[16:]], axis=0)
        send1[iteration] = (spectrum * scale).astype(BF16).reshape(N_SLAB, 2, 128)
        moving = exchange(send1, recv1, iteration, 0)
        sent.append(moving[1])

        if iteration == 0:
            await_shots((0, 3))
            full_covers((0, 1, 3))
            side_covers()
            make_filter()
        slab = const("slab")
        small = const("small")
        twists = const("twists")
        arrived(moving)
        lines = recv1[iteration].reshape(2 * N_SLAB, 128)
        both = mm(slab[0], lines) + mm(slab[1], lines)
        part = sign * both[:256]
        other = swap_parts(both[256:])
        turned = []
        for value in (sign * (part + other), part - other):
            turned.append(value * twists[0] + swap_parts(value) * twists[1])
        high, low = split(jnp.concatenate(turned, axis=0))
        value = mm(high, small[0]) + mm(low, small[0]) + mm(high, small[1])
        line, mirror = value[:256], value[256:]
        cross = mix[...]
        value = jnp.concatenate(
            [line * filt[0] + mirror * cross, mirror * filt[1] + line * cross], axis=0
        )
        high, low = split(value)
        value = mm(high, small[2]) + mm(low, small[2]) + mm(high, small[3])
        turned = []
        for part in (value[:256], value[256:]):
            turned.append(part * twists[2] - swap_parts(part) * twists[3])
        line, mirror = turned[0], sign * turned[1]
        high, low = split(line + mirror)
        both = mm(slab[0, 0:256], jnp.concatenate([high, low], axis=1))
        real_part = both[:, :128] + both[:, 128:] + mm(slab[1, 0:256], high)
        high, low = split(line - mirror)
        both = mm(slab[0, 256:512], jnp.concatenate([high, low], axis=1))
        imag_part = both[:, :128] + both[:, 128:] + mm(slab[1, 256:512], high)
        send2[iteration] = (
            (real_part - sign * swap_parts(imag_part)).astype(BF16).reshape(N_SLAB, 2, 128)
        )
        moving = exchange(send2, recv2, iteration, 1)
        sent.append(moving[1])

        row_pos = (
            lax.broadcasted_iota(jnp.int32, (3 * ROWS, SLOTS), 0) + (s * ROWS - ROWS)
        ).astype(F32)
        for d in range(4):
            lanes = slice(d * SLOTS, (d + 1) * SLOTS)
            for place, step in enumerate((0, 3, 1)):
                slot = 4 * d + lax.rem(c + step, N_COL)
                inside = (row_pos >= shots[slot, 0:1, :]) & (row_pos < shots[slot, 1:2, :])
                value = jnp.where(inside, dose_of(slot), 0.0).astype(BF16)
                if place:
                    weights_side[place - 1, :, lanes] = value
                else:
                    weights[:, lanes] = value
        rows_band = const("rows_band")
        cols_band = const("cols_band")
        for side in range(2):
            at = side * (COLS + 128)
            block = mm(weights_side[side], cover_side[side]).astype(BF16)
            across[:, at : at + 128] = mm(rows_band[...], block).astype(BF16)

        def raster(block, carry):
            at = pl.multiple_of(block * 256, 256)
            tile = mm(weights[...], cover[:, pl.ds(at, 256)]).astype(BF16)
            across[:, pl.ds(at + 128, 256)] = mm(rows_band[...], tile).astype(BF16)
            return carry

        lax.fori_loop(0, COLS // 256, raster, 0)

        def blur(block, carry):
            at = pl.multiple_of(block * 128, 128)
            short[:, pl.ds(at, 128)] = mm(across[:, pl.ds(at, 384)], cols_band[...])
            return carry

        lax.fori_loop(0, COLS // 128, blur, 0)
        row_twice = const("row_twice")
        col_twice = const("col_twice")
        arrived(moving)

        held = recv2[iteration].reshape(2 * N_SLAB, 128)
        both = mm(held, column[0], ((0,), (0,))) + mm(held, column[1], ((0,), (0,)))
        nyquist = mm(held[0:16], alternate[...], ((0,), (0,)))[64:96]
        points = []
        for place in range(2):
            re = slice(place * 32, place * 32 + 32)
            im = slice(place * 32 + 64, place * 32 + 96)
            points.append(
                (both[re, :512] - both[im, 512:], both[re, 512:] + both[im, :512])
            )
        points[0] = (points[0][0] + jnp.where(c == 0, nyquist, 0.0), points[0][1])

        x_copies = []
        for step in (2, 1, 3, 0):
            quarter = lax.rem(c + step, N_COL)
            for half in range(2):
                at = pl.multiple_of(quarter * 1024 + half * 512, 512)
                total = jnp.zeros((32, 512), F32)
                for place in range(2):
                    total = total + (
                        points[place][0] * classes[2 * place : 2 * place + 1, pl.ds(at, 512)]
                        - points[place][1]
                        * classes[2 * place + 1 : 2 * place + 2, pl.ds(at, 512)]
                    )
                field_out[iteration, step, :, half * 512 : (half + 1) * 512] = total.astype(BF16)
            if step:
                copy = remote(
                    field_out.at[iteration, step],
                    field.at[iteration, step],
                    x_send.at[iteration, step],
                    x_recv.at[iteration, step],
                    (s, quarter),
                )
                copy.start()
                x_copies.append(copy)
        back = field_out[iteration, 0].astype(F32)
        for step, copy in zip((2, 1, 3), x_copies):
            copy.wait_recv()
            back = back + field[iteration, step].astype(F32)
        row = lax.broadcasted_iota(jnp.int32, (32, 1024), 0).astype(F32)
        back = back * jnp.exp(row * (-math.log(2.0) / 32.0))

        high, low = split(back)
        high = mm(row_twice[...], high).astype(BF16)
        low = mm(row_twice[...], low).astype(BF16)
        pieces = [slice(block * 128, (block + 1) * 128) for block in range(8)]
        stacked = jnp.concatenate(
            [jnp.concatenate([high[:, p], low[:, p]], axis=1) for p in pieces], axis=0
        )
        twice = mm(stacked, col_twice[...])
        for block in range(8):
            wide = slice(block * 256, (block + 1) * 256)
            value = short[:, wide] + twice[block * ROWS : (block + 1) * ROWS]
            if iteration == ITERS - 1:
                exposure_ref[:, wide] = value
            exposure_bf[:, wide] = value.astype(BF16)

        measured = mm(exposure_bf[...], cover[SLOTS : 3 * SLOTS, :], ((1,), (1,)))
        row_pos = (lax.broadcasted_iota(jnp.int32, (ROWS, SLOTS), 0) + s * ROWS).astype(F32)
        for d in (1, 2):
            slot = 4 * d + c
            inside = (row_pos >= shots[slot, 0:1, :]) & (row_pos < shots[slot, 1:2, :])
            part = jnp.where(inside, measured[:, (d - 1) * SLOTS : d * SLOTS], 0.0)
            sums_out[iteration, d - 1 : d, :] = jnp.sum(part, axis=0, keepdims=True)
        sent.extend(x_copies)
        if iteration == 0:
            for offset in (2, -2, 1, -1, 0):
                for step in range(N_COL):
                    if offset or step:
                        copy = remote(
                            sums_out.at[iteration],
                            sums.at[4 * (2 - offset) + c],
                            sums_send.at[4 * (2 - offset) + step],
                            sums_recv.at[4 * (2 - offset) + c],
                            near(offset, lax.rem(c + step, N_COL)),
                        )
                        copy.start()
                        sent.append(copy)
            sums[8 + c] = sums_out[iteration]
            for place in range(5):
                for step in range(N_COL):
                    if place != 2 or step:
                        slot = 4 * place + lax.rem(c + step, N_COL)
                        remote(
                            sums_out.at[iteration],
                            sums.at[slot],
                            sums_send.at[0],
                            sums_recv.at[slot],
                            (s, c),
                        ).wait_recv()
            for slot in range(4 * N_COL):
                box = shots[slot]
                whole_area = (box[1:2] - box[0:1]) * (box[3:4] - box[2:3])
                average = (sums[slot, 1:2, :] + sums[slot + N_COL, 0:1, :]) / whole_area
                past = box[4:5]
                doses[slot] = jnp.where(
                    past > 0.0, past * jnp.exp(RELAX * (TARGET_LEVEL - average)), 0.0
                )
        else:
            copy = remote(
                sums_out.at[iteration],
                spill,
                spill_sems.at[0],
                spill_sems.at[1],
                near(-1, c),
            )
            copy.start()
            for other in sent:
                other.wait_send()
            for other in shot_copies:
                other.wait_send()
            for away, other in t_copies:

                @pl.when(away)
                def _(other=other):
                    other.wait_send()

            copy.wait()
            average = (sums_out[iteration, 1:2, :] + spill[0:1, :]) / area
            dose = doses[8 + c]
            dose = jnp.where(live, dose * jnp.exp(RELAX * (TARGET_LEVEL - average)), 0.0)
            dosage_ref[...] = dose.reshape(SLOTS)


def per_device(shot_boxes, shot_counts, shot_doses, transfer):
    t = tables()
    constants = [jnp.asarray(t[name]) for name in NAMES]
    vmem = pl.BlockSpec(memory_space=pltpu.VMEM)
    stay = pl.BlockSpec(memory_space=pl.ANY)
    dma = pltpu.SemaphoreType.DMA
    held = [
        pltpu.VMEM(value.shape[1:] if name == "classes" else value.shape, value.dtype)
        for name, value in zip(NAMES, constants)
    ]
    dosage, exposure = pl.pallas_call(
        kernel,
        out_shape=(
            jax.ShapeDtypeStruct((SLOTS,), F32),
            jax.ShapeDtypeStruct((ROWS, COLS), F32),
        ),
        in_specs=[stay] * (4 + len(constants)),
        out_specs=(vmem, vmem),
        scratch_shapes=[
            *held,
            pltpu.VMEM((4, SLOTS), jnp.int32),
            pltpu.VMEM((1, 1), jnp.int32),
            pltpu.VMEM((1, SLOTS), F32),
            pltpu.VMEM((8, SLOTS), F32),
            pltpu.VMEM((16, 8, SLOTS), F32),
            pltpu.VMEM((16, 1, SLOTS), F32),
            pltpu.VMEM((ITERS, 2, SLOTS), F32),
            pltpu.VMEM((20, 2, SLOTS), F32),
            pltpu.VMEM((2, SLOTS), F32),
            pltpu.VMEM((8, 1, LONG), F32),
            pltpu.VMEM((2, 256, 128), F32),
            pltpu.VMEM((256, 128), F32),
            pltpu.VMEM((4 * SLOTS, COLS), BF16),
            pltpu.VMEM((2, 4 * SLOTS, 128), BF16),
            pltpu.VMEM((N_COL, 2 * SLOTS, 256), BF16),
            pltpu.VMEM((3 * ROWS, 4 * SLOTS), BF16),
            pltpu.VMEM((2, 3 * ROWS, 4 * SLOTS), BF16),
            pltpu.VMEM((ROWS, COLS + 256), BF16),
            pltpu.VMEM((ROWS, COLS), F32),
            pltpu.VMEM((ROWS, COLS), BF16),
            pltpu.VMEM((32, LONG), F32),
            pltpu.VMEM((256, 1024), BF16),
            pltpu.VMEM((ITERS, N_SLAB, 2, 128), BF16),
            pltpu.VMEM((ITERS, N_SLAB, 2, 128), BF16),
            pltpu.VMEM((ITERS, N_SLAB, 2, 128), BF16),
            pltpu.VMEM((ITERS, N_SLAB, 2, 128), BF16),
            pltpu.VMEM((ITERS, N_COL, 32, 1024), BF16),
            pltpu.VMEM((ITERS, N_COL, 32, 1024), BF16),
            dma((len(NAMES),)),
            dma((3,)),
            dma((16,)),
            dma((16,)),
            dma((20,)),
            dma((20,)),
            dma((8,)),
            dma((8,)),
            dma((2 * ITERS,)),
            dma((2 * ITERS,)),
            dma((2 * ITERS,)),
            dma((ITERS, N_COL)),
            dma((ITERS, N_COL)),
            dma((2,)),
        ],
        compiler_params=pltpu.CompilerParams(
            collective_id=0, has_side_effects=True, vmem_limit_bytes=60 << 20
        ),
        name="dose_correction",
    )(shot_boxes, shot_counts, shot_doses.reshape(1, SLOTS), transfer, *constants)
    return dosage, exposure


def solution(mesh):
    placed = (
        P(None, ("slab", "col")),
        P("slab", "col"),
        P(("slab", "col")),
        P(("slab", "col"), None),
    )
    return jax.shard_map(
        per_device,
        mesh=mesh,
        in_specs=placed,
        out_specs=(P(("slab", "col")), P("slab", "col")),
        check_vma=False,
    )
```

```python
import functools
import math

import jax
import jax.numpy as jnp
import numpy as np
from jax import lax
from jax.experimental import pallas as pl
from jax.experimental.pallas import tpu as pltpu
from jax.sharding import PartitionSpec as P

HALO = 64
ITERS = 2
SLOTS = 256
ROWS = 64
COLS = 2048
LONG = 4096
N_SLAB = 128
N_COL = 4
RELAX = 0.5
TARGET_LEVEL = 1.0
F32 = jnp.float32
BF16 = jnp.bfloat16
MESH = pl.DeviceIdType.MESH


def halves(values):
    high = np.asarray(values, np.float32).astype(jnp.bfloat16)
    low = (np.asarray(values, np.float64) - high.astype(np.float64)).astype(jnp.bfloat16)
    return high, low


def joined(high, low):
    return np.block([[high, low], [high, np.zeros_like(low)]])


def blur_taps():
    pos = np.arange(-HALO, HALO + 1).astype(np.float32)
    spread = np.float32(HALO / 3.0)
    raw = np.exp(np.float32(-0.5) * pos * pos / (spread * spread)).astype(np.float32)
    return (raw / raw.sum(dtype=np.float32)).astype(jnp.bfloat16)


@functools.lru_cache(None)
def tables():
    turn = 2.0 * np.pi
    angle = turn / 512 * ((np.arange(256)[:, None] * np.arange(512)[None, :]) % 512)
    column = np.concatenate([np.cos(angle), np.sin(angle)], axis=1)
    slab_angle = turn / 128 * ((np.arange(128)[:, None] * np.arange(128)[None, :]) % 128)
    pair = np.eye(2)
    slab = np.concatenate([np.kron(np.cos(slab_angle), pair), np.kron(np.sin(slab_angle), pair)])
    small = turn / 32 * ((np.arange(32)[:, None] * np.arange(32)[None, :]) % 32)
    cos, sin = np.cos(small), np.sin(small)
    cos, sin = np.kron(pair, cos), np.kron(pair, sin)
    forward = np.block([[cos, -sin], [sin, cos]])
    backward = np.block([[cos, sin], [-sin, cos]]) * 4.0 ** ((np.arange(128) % 32) / 32.0)
    lane = np.arange(128)
    scale = 2.0 ** ((lane % 32) / 32.0)
    twist = turn / LONG * np.repeat(np.arange(128), 2)[:, None] * (lane % 32)[None, :]
    sign = np.where(lane < 64, 1.0, -1.0)
    twists = np.stack(
        [
            np.cos(twist) / scale,
            np.sin(twist) * sign / scale,
        ]
    ).astype(np.float32)
    classes = np.zeros((N_COL, 4, LONG), np.float32)
    for col in range(N_COL):
        for place, k in enumerate((col, col + 2048) if col else (0, 4)):
            theta = turn / LONG * ((np.arange(LONG) * k) % LONG)
            classes[col, 2 * place] = np.cos(theta)
            classes[col, 2 * place + 1] = np.sin(theta)
    taps = blur_taps()
    rows_band = np.zeros((ROWS, ROWS + 2 * HALO), jnp.bfloat16)
    for r in range(ROWS):
        rows_band[r, r : r + 2 * HALO + 1] = taps
    cols_band = np.zeros((384, 128), jnp.bfloat16)
    for c in range(128):
        cols_band[c + 64 : c + 64 + 2 * HALO + 1, c] = taps
    row_twice = (np.arange(ROWS)[:, None] // 2 == np.arange(32)[None, :]).astype(jnp.bfloat16)
    col_twice = (np.arange(256)[:, None] % 128 == np.arange(256)[None, :] // 2).astype(
        jnp.bfloat16
    )
    alternate = np.zeros((16, 512), jnp.bfloat16)
    alternate[0] = 1 - 2 * (np.arange(512) % 2)
    scales = np.stack([scale, np.zeros(128)] * 4).astype(np.float32)
    return dict(
        column=np.stack(halves(column)),
        slab=np.stack(halves(slab)),
        small=np.stack([joined(*halves(forward)), joined(*halves(backward))]),
        twists=twists,
        classes=classes,
        rows_band=rows_band,
        cols_band=cols_band,
        row_twice=row_twice,
        col_twice=col_twice,
        alternate=alternate,
        scales=scales,
    )


NAMES = (
    "column",
    "slab",
    "small",
    "twists",
    "classes",
    "rows_band",
    "cols_band",
    "row_twice",
    "col_twice",
    "alternate",
    "scales",
)


def mm(a, b, dims=((1,), (0,))):
    return lax.dot_general(a, b, (dims, ((), ())), preferred_element_type=F32)


def split(x):
    high = x.astype(BF16)
    return high, (x - high.astype(F32)).astype(BF16)


def swap_parts(x):
    return pltpu.roll(x, 64, 1)


def around(place):
    return jnp.where(place >= N_SLAB, place - N_SLAB, place)


def over_slabs(act):
    def turn(group, carry):
        for place in range(8):
            act(group * 8 + place)
        return carry

    lax.fori_loop(6, 16, turn, 0)
    lax.fori_loop(1, 6, turn, 0)
    for step in range(1, 8):
        act(step)


def kernel(
    boxes_in,
    counts_in,
    doses_in,
    transfer_ref,
    *rest,
):
    constants_in = dict(zip(NAMES, rest[: len(NAMES)]))
    rest = rest[len(NAMES) :]
    dosage_ref, exposure_ref = rest[:2]
    held_in = dict(zip(NAMES, rest[2 : 2 + len(NAMES)]))
    (
        boxes,
        counts,
        doses_own,
        pack,
        shots,
        doses,
        sums_out,
        sums,
        spill,
        t_rows,
        filt,
        mix,
        cover,
        cover_side,
        cover_pool,
        weights,
        weights_side,
        across,
        short,
        exposure_bf,
        coarse,
        uv,
        send1,
        recv1,
        send2,
        recv2,
        field_out,
        field,
        const_sems,
        in_sems,
        shot_send,
        shot_recv,
        sums_send,
        sums_recv,
        t_send,
        t_recv,
        slab_send,
        slab_recv,
        own_sems,
        x_send,
        x_recv,
        spill_sems,
    ) = rest[2 + len(NAMES) :]
    s = lax.axis_index("slab")
    c = lax.axis_index("col")

    in_copies = [
        pltpu.make_async_copy(source, target, in_sems.at[at])
        for at, (source, target) in enumerate(
            ((boxes_in, boxes), (counts_in, counts), (doses_in, doses_own))
        )
    ]
    for copy in in_copies:
        copy.start()
    const_copies = {}
    for at, name in enumerate(NAMES):
        source = constants_in[name]
        source = source.at[c] if name == "classes" else source
        const_copies[name] = pltpu.make_async_copy(source, held_in[name], const_sems.at[at])
        const_copies[name].start()

    def near(offset, col):
        return (lax.rem(s + offset + N_SLAB, N_SLAB), col)

    def remote(src, dst, send_sem, recv_sem, device):
        return pltpu.make_async_remote_copy(
            src_ref=src,
            dst_ref=dst,
            send_sem=send_sem,
            recv_sem=recv_sem,
            device_id=device,
            device_id_type=MESH,
        )

    here = 4 * s + c
    upper = s // 64

    def t_target(k):
        if k in (1, 2, 3):
            m, place, opposite, col = here % 256, upper, 0, k
        elif k in (5, 6, 7):
            m, place, opposite, col = (511 - here) % 256, 1 - upper, 1, 8 - k
        elif k == 4:
            m, place, opposite, col = here + upper * (511 - 2 * here), 1, upper, 0
        else:
            m, place, opposite, col = (here + upper * (512 - 2 * here)) % 256, 0, upper, 0
        return m // 2, col, 4 * (m % 2) + 2 * place + opposite

    def t_source(pp, place, opposite):
        p = 2 * s + pp
        if opposite:
            other = 511 - (p + 256 * place)
            zero_col = 511 - p if place else 512 - p - 256 * jnp.where(p == 0, 1, 0)
        else:
            other = p + 256 * place
            zero_col = p
        m = jnp.where(c == 0, zero_col, other)
        return m // 4, m % 4

    barrier = pltpu.get_barrier_semaphore()

    def greet(step):
        pl.semaphore_signal(
            barrier,
            inc=1,
            device_id=(around(s + step), c),
            device_id_type=MESH,
        )

    over_slabs(greet)
    for offset in range(-2, 3):
        for step in range(1, N_COL):
            pl.semaphore_signal(
                barrier,
                inc=1,
                device_id=near(offset, lax.rem(c + step, N_COL)),
                device_id_type=MESH,
            )
    for pp in range(2):
        for place in range(2):
            for opposite in range(2):
                from_slab, from_col = t_source(pp, place, opposite)
                away = 4 * from_slab + from_col != here

                @pl.when(away)
                def _(device=(from_slab, from_col)):
                    pl.semaphore_signal(barrier, inc=1, device_id=device, device_id_type=MESH)

    for copy in in_copies:
        copy.wait()
    box_own = boxes[...].astype(F32)
    slot_id = lax.broadcasted_iota(jnp.int32, (1, SLOTS), 1)
    dose = jnp.where(slot_id < counts[...], doses_own[...], 0.0)
    pack[0:4, :] = box_own
    pack[4:8, :] = jnp.broadcast_to(dose, (4, SLOTS))
    shots[8 + c] = pack[...]

    def from_block(col):
        begins, ends, firsts = [], [], []
        for d in (1, 2):
            box = shots[4 * d + col]
            begin = box[2:3] - (col * COLS).astype(F32)
            first = jnp.floor(begin * (1.0 / 256.0))
            begins.append(begin - first * 256.0 - 64.0)
            ends.append(box[3:4] - (col * COLS).astype(F32) - first * 256.0 - 64.0)
            firsts.append(first)
        return tuple(jnp.concatenate(parts, axis=1) for parts in (begins, ends, firsts))

    def pool_cover(col, carry):
        begin, end, _ = from_block(col)
        row = lax.broadcasted_iota(jnp.int32, (16, 2 * SLOTS), 0)
        both = jnp.where(row == 0, begin, jnp.where(row == 1, end, 0.0)).astype(BF16)
        row = lax.broadcasted_iota(jnp.int32, (16, 256), 0)
        lane = lax.broadcasted_iota(jnp.int32, (16, 256), 1)
        pick = jnp.where(row == lane // 128, 1.0, 0.0).astype(BF16)
        wide = mm(both, pick, ((0,), (0,)))
        begin, end = wide[:, :128], wide[:, 128:]
        for part in range(2):
            lane = lax.broadcasted_iota(jnp.int32, (2 * SLOTS, 128), 1)
            left = (2 * lane + (256 * part - 64)).astype(F32)
            inside = jnp.minimum(end, left + 2.0) - jnp.maximum(begin, left)
            cover_pool[col, :, part * 128 : (part + 1) * 128] = jnp.maximum(inside, 0.0).astype(
                BF16
            )
        return carry

    def full_covers(ds):
        for d in ds:
            box = jnp.transpose(shots[4 * d + c])
            start = jnp.broadcast_to(box[:, 2:3], (SLOTS, 128))
            end = jnp.broadcast_to(box[:, 3:4], (SLOTS, 128))
            rows = slice(d * SLOTS, (d + 1) * SLOTS)

            def one(block, inner):
                lane = lax.broadcasted_iota(jnp.int32, (SLOTS, 128), 1) + block * 128
                pos = (lane + c * COLS).astype(F32)
                inside = (pos >= start) & (pos < end)
                at = pl.multiple_of(block * 128, 128)
                cover[rows, pl.ds(at, 128)] = jnp.where(inside, 1.0, 0.0).astype(BF16)
                return inner

            lax.fori_loop(0, COLS // 128, one, 0)

    def side_covers():
        for d in range(4):
            rows = slice(d * SLOTS, (d + 1) * SLOTS)
            for side in range(2):
                other = lax.rem(c + (1 if side else 3), N_COL)
                box = jnp.transpose(shots[4 * d + other])
                lane = lax.broadcasted_iota(jnp.int32, (SLOTS, 128), 1)
                pos = (lane + c * COLS + (COLS if side else -128)).astype(F32)
                inside = (pos >= box[:, 2:3]) & (pos < box[:, 3:4])
                cover_side[side, rows, :] = jnp.where(inside, 1.0, 0.0).astype(BF16)

    full_covers((2,))

    expected = 15 + N_SLAB - 1
    for k in range(8):
        to_slab, to_col, _ = t_target(k)
        expected = expected + jnp.where(4 * to_slab + to_col != here, 1, 0)
    pl.semaphore_wait(barrier, expected)

    shot_copies = []
    for d in range(4):
        for step in range(N_COL):
            if d != 2 or step:
                shot_copies.append(
                    remote(
                        pack,
                        shots.at[4 * d + c],
                        shot_send.at[4 * d + step],
                        shot_recv.at[4 * d + c],
                        near(2 - d, lax.rem(c + step, N_COL)),
                    )
                )
    for copy in shot_copies:
        copy.start()

    t_copies = []
    for k in range(8):
        to_slab, to_col, slot = t_target(k)
        away = 4 * to_slab + to_col != here
        row = transfer_ref.at[pl.ds(k, 1)]
        distant = remote(row, t_rows.at[slot], t_send.at[k], t_recv.at[slot], (to_slab, to_col))
        local = pltpu.make_async_copy(row, t_rows.at[slot], t_recv.at[slot])
        t_copies.append((away, distant))

        @pl.when(away)
        def _(copy=distant):
            copy.start()

        @pl.when(jnp.logical_not(away))
        def _(copy=local):
            copy.start()

    def await_shots(ds):
        for d in ds:
            for step in range(N_COL):
                if d != 2 or step:
                    slot = 4 * d + lax.rem(c + step, N_COL)
                    remote(
                        pack, shots.at[slot], shot_send.at[0], shot_recv.at[slot], (s, c)
                    ).wait_recv()

    await_shots((1, 2))

    lax.fori_loop(0, N_COL, pool_cover, 0)

    def blocks(row):
        return jnp.concatenate([row[:, b * 128 : (b + 1) * 128] for b in range(32)], axis=0)

    def make_filter():
        for slot in range(8):
            remote(
                transfer_ref.at[pl.ds(0, 1)],
                t_rows.at[slot],
                t_send.at[0],
                t_recv.at[slot],
                (s, c),
            ).wait_recv()
        unit = 1.0 / (LONG * LONG)
        lane = lax.broadcasted_iota(jnp.int32, (128, 128), 1)
        shared = jnp.where((lane % 64 < 32) & (here == 0), 1.0, 0.0)
        for pp in range(2):
            tables_of = []
            for opposite in range(2):
                first = blocks(t_rows[4 * pp + opposite])
                second = blocks(t_rows[4 * pp + 2 + opposite])
                stack = jnp.concatenate([first, second, first, second], axis=0)
                tables_of.append(jnp.transpose(stack) * unit)
            plus, minus = tables_of
            cross = jnp.zeros((128, 128), F32)
            if pp == 0:
                mean = 0.25 * (plus + minus)
                cross = 0.25 * (plus - minus) * shared
                plus = jnp.where(shared > 0.0, mean, plus)
                minus = jnp.where(shared > 0.0, mean, minus)
            filt[0, pl.ds(pp, 128, stride=2), :] = plus
            filt[1, pl.ds(pp, 128, stride=2), :] = minus
            mix[pl.ds(pp, 128, stride=2), :] = cross

    live = dose > 0.0
    area = (box_own[1:2] - box_own[0:1]) * (box_own[3:4] - box_own[2:3])

    def exchange(source, target, iteration, which):
        lane = which * ITERS + iteration

        def go(step):
            there = around(s + step)
            remote(
                source.at[iteration, there],
                target.at[iteration, s],
                slab_send.at[lane],
                slab_recv.at[lane],
                (there, c),
            ).start()

        over_slabs(go)
        own = pltpu.make_async_copy(
            source.at[iteration, s],
            target.at[iteration, s],
            own_sems.at[lane],
        )
        own.start()
        whole = remote(
            source.at[iteration, pl.ds(0, N_SLAB - 1)],
            target.at[iteration, pl.ds(0, N_SLAB - 1)],
            slab_send.at[lane],
            slab_recv.at[lane],
            (lax.rem(s + 1, N_SLAB), c),
        )
        return own, whole

    def arrived(pair):
        own, whole = pair
        own.wait()
        whole.wait_recv()

    lane_id = lax.broadcasted_iota(jnp.int32, (256, 128), 1)
    sign = jnp.where(lane_id < 64, 1.0, -1.0)
    sent = []
    ready = set()

    def const(name):
        if name not in ready:
            ready.add(name)
            const_copies[name].wait()
        return held_in[name]

    for iteration in range(ITERS):

        def dose_of(slot):
            value = shots[slot, 4:5, :] if iteration == 0 else doses[slot]
            return value.astype(BF16).astype(F32)

        for col in range(N_COL):
            parts = []
            for d in (1, 2):
                slot = 4 * d + col
                top = 2 * lax.broadcasted_iota(jnp.int32, (32, SLOTS), 0) + s * ROWS
                top = top.astype(F32)
                part = jnp.minimum(shots[slot, 1:2, :], top + 2.0) - jnp.maximum(
                    shots[slot, 0:1, :], top
                )
                parts.append(jnp.maximum(part, 0.0) * (dose_of(slot) * 0.25))
            row_part = jnp.concatenate(parts, axis=1)
            first = from_block(jnp.int32(col))[2]
            placed = jnp.concatenate(
                [
                    (row_part * jnp.where(first == float(b), 1.0, 0.0)).astype(BF16)
                    for b in range(8)
                ],
                axis=0,
            )
            tile = mm(placed, cover_pool[col])
            for b in range(8):
                at = col * 1024 + b * 128
                block = tile[b * 32 : (b + 1) * 32, :128]
                if b:
                    block = block + tile[(b - 1) * 32 : b * 32, 128:]
                coarse[:, at : at + 128] = block

        classes = const("classes")
        for place in range(2):
            real = jnp.zeros((32, 512), F32)
            imag = jnp.zeros((32, 512), F32)
            for q in range(8):
                block = slice(q * 512, (q + 1) * 512)
                x = coarse[:, block]
                real = real + x * classes[2 * place : 2 * place + 1, block]
                imag = imag - x * classes[2 * place + 1 : 2 * place + 2, block]
            at = place * 32
            real_high, real_low = split(real)
            imag_high, imag_low = split(imag)
            for base, re, im in ((at, real_high, imag_high), (128 + at, real_low, imag_low)):
                uv[base : base + 32, 0:512] = re
                uv[base + 64 : base + 96, 0:512] = im
                uv[base : base + 32, 512:1024] = im
                uv[base + 64 : base + 96, 512:1024] = -re
        column = const("column")
        both = mm(column[0], uv[...], ((1,), (1,)))
        spectrum = both[:, :128] + both[:, 128:] + mm(column[1], uv[0:128, :], ((1,), (1,)))
        alternate = const("alternate")
        both = mm(alternate[...], uv[:, 512:1024], ((1,), (1,)))
        nyquist = both[:, :128] + both[:, 128:]
        lane16 = lax.broadcasted_iota(jnp.int32, (16, 128), 1)
        chosen = (lane16 >= 64) & (lane16 < 96) & (c == 0)
        nyquist = jnp.where(chosen, nyquist, 0.0)
        scales = const("scales")
        scale = scales[0:1, :]
        spectrum = jnp.concatenate([spectrum[0:16] - nyquist, spectrum[16:]], axis=0)
        send1[iteration] = (spectrum * scale).astype(BF16).reshape(N_SLAB, 2, 128)
        moving = exchange(send1, recv1, iteration, 0)
        sent.append(moving[1])

        if iteration == 0:
            await_shots((0, 3))
            full_covers((0, 1, 3))
            side_covers()
            make_filter()
        slab = const("slab")
        small = const("small")
        twists = const("twists")
        arrived(moving)
        lines = recv1[iteration].reshape(2 * N_SLAB, 128)
        both = mm(slab[0], lines) + mm(slab[1], lines)
        part = sign * both[:256]
        other = swap_parts(both[256:])
        turned = []
        for value in (sign * (part + other), part - other):
            turned.append(value * twists[0] + swap_parts(value) * twists[1])
        value = mm(jnp.concatenate(split(jnp.concatenate(turned, axis=0)), axis=1), small[0])
        value = value[:, :128] + value[:, 128:]
        line, mirror = value[:256], value[256:]
        cross = mix[...]
        value = jnp.concatenate(
            [line * filt[0] + mirror * cross, mirror * filt[1] + line * cross], axis=0
        )
        value = mm(jnp.concatenate(split(value), axis=1), small[1])
        value = value[:, :128] + value[:, 128:]
        turned = []
        for part in (value[:256], value[256:]):
            turned.append(part * twists[0] - swap_parts(part) * twists[1])
        line, mirror = turned[0], sign * turned[1]
        high, low = split(line + mirror)
        both = mm(slab[0, 0:256], jnp.concatenate([high, low], axis=1))
        real_part = both[:, :128] + both[:, 128:] + mm(slab[1, 0:256], high)
        high, low = split(line - mirror)
        both = mm(slab[0, 256:512], jnp.concatenate([high, low], axis=1))
        imag_part = both[:, :128] + both[:, 128:] + mm(slab[1, 256:512], high)
        send2[iteration] = (
            (real_part - sign * swap_parts(imag_part)).astype(BF16).reshape(N_SLAB, 2, 128)
        )
        moving = exchange(send2, recv2, iteration, 1)
        sent.append(moving[1])

        row_pos = (
            lax.broadcasted_iota(jnp.int32, (3 * ROWS, SLOTS), 0) + (s * ROWS - ROWS)
        ).astype(F32)
        for d in range(4):
            lanes = slice(d * SLOTS, (d + 1) * SLOTS)
            for place, step in enumerate((0, 3, 1)):
                slot = 4 * d + lax.rem(c + step, N_COL)
                inside = (row_pos >= shots[slot, 0:1, :]) & (row_pos < shots[slot, 1:2, :])
                value = jnp.where(inside, dose_of(slot), 0.0).astype(BF16)
                if place:
                    weights_side[place - 1, :, lanes] = value
                else:
                    weights[:, lanes] = value
        rows_band = const("rows_band")
        cols_band = const("cols_band")
        for side in range(2):
            at = side * (COLS + 128)
            block = mm(weights_side[side], cover_side[side]).astype(BF16)
            across[:, at : at + 128] = mm(rows_band[...], block).astype(BF16)

        def raster(block, carry):
            at = pl.multiple_of(block * 256, 256)
            tile = mm(weights[...], cover[:, pl.ds(at, 256)]).astype(BF16)
            across[:, pl.ds(at + 128, 256)] = mm(rows_band[...], tile).astype(BF16)
            return carry

        lax.fori_loop(0, COLS // 256, raster, 0)

        def blur(block, carry):
            at = pl.multiple_of(block * 128, 128)
            short[:, pl.ds(at, 128)] = mm(across[:, pl.ds(at, 384)], cols_band[...])
            return carry

        lax.fori_loop(0, COLS // 128, blur, 0)
        row_twice = const("row_twice")
        col_twice = const("col_twice")
        arrived(moving)

        held = recv2[iteration].reshape(2 * N_SLAB, 128)
        both = mm(held, column[0], ((0,), (0,))) + mm(held, column[1], ((0,), (0,)))
        nyquist = mm(held[0:16], alternate[...], ((0,), (0,)))[64:96]
        points = []
        for place in range(2):
            re = slice(place * 32, place * 32 + 32)
            im = slice(place * 32 + 64, place * 32 + 96)
            points.append(
                (both[re, :512] - both[im, 512:], both[re, 512:] + both[im, :512])
            )
        points[0] = (points[0][0] + jnp.where(c == 0, nyquist, 0.0), points[0][1])

        x_copies = []
        for step in (2, 1, 3, 0):
            quarter = lax.rem(c + step, N_COL)
            for half in range(2):
                at = pl.multiple_of(quarter * 1024 + half * 512, 512)
                total = jnp.zeros((32, 512), F32)
                for place in range(2):
                    total = total + (
                        points[place][0] * classes[2 * place : 2 * place + 1, pl.ds(at, 512)]
                        - points[place][1]
                        * classes[2 * place + 1 : 2 * place + 2, pl.ds(at, 512)]
                    )
                field_out[iteration, step, :, half * 512 : (half + 1) * 512] = total.astype(BF16)
            if step:
                copy = remote(
                    field_out.at[iteration, step],
                    field.at[iteration, step],
                    x_send.at[iteration, step],
                    x_recv.at[iteration, step],
                    (s, quarter),
                )
                copy.start()
                x_copies.append(copy)
        back = field_out[iteration, 0].astype(F32)
        for step, copy in zip((2, 1, 3), x_copies):
            copy.wait_recv()
            back = back + field[iteration, step].astype(F32)
        row = lax.broadcasted_iota(jnp.int32, (32, 1024), 0).astype(F32)
        back = back * jnp.exp(row * (-math.log(2.0) / 32.0))

        high, low = split(back)
        high = mm(row_twice[...], high).astype(BF16)
        low = mm(row_twice[...], low).astype(BF16)
        pieces = [slice(block * 128, (block + 1) * 128) for block in range(8)]
        stacked = jnp.concatenate(
            [jnp.concatenate([high[:, p], low[:, p]], axis=1) for p in pieces], axis=0
        )
        twice = mm(stacked, col_twice[...])
        for block in range(8):
            wide = slice(block * 256, (block + 1) * 256)
            value = short[:, wide] + twice[block * ROWS : (block + 1) * ROWS]
            if iteration == ITERS - 1:
                exposure_ref[:, wide] = value
            exposure_bf[:, wide] = value.astype(BF16)

        measured = mm(exposure_bf[...], cover[SLOTS : 3 * SLOTS, :], ((1,), (1,)))
        row_pos = (lax.broadcasted_iota(jnp.int32, (ROWS, SLOTS), 0) + s * ROWS).astype(F32)
        for d in (1, 2):
            slot = 4 * d + c
            inside = (row_pos >= shots[slot, 0:1, :]) & (row_pos < shots[slot, 1:2, :])
            part = jnp.where(inside, measured[:, (d - 1) * SLOTS : d * SLOTS], 0.0)
            sums_out[iteration, d - 1 : d, :] = jnp.sum(part, axis=0, keepdims=True)
        sent.extend(x_copies)
        if iteration == 0:
            for offset in (2, -2, 1, -1, 0):
                for step in range(N_COL):
                    if offset or step:
                        copy = remote(
                            sums_out.at[iteration],
                            sums.at[4 * (2 - offset) + c],
                            sums_send.at[4 * (2 - offset) + step],
                            sums_recv.at[4 * (2 - offset) + c],
                            near(offset, lax.rem(c + step, N_COL)),
                        )
                        copy.start()
                        sent.append(copy)
            sums[8 + c] = sums_out[iteration]
            for place in range(5):
                for step in range(N_COL):
                    if place != 2 or step:
                        slot = 4 * place + lax.rem(c + step, N_COL)
                        remote(
                            sums_out.at[iteration],
                            sums.at[slot],
                            sums_send.at[0],
                            sums_recv.at[slot],
                            (s, c),
                        ).wait_recv()
            for slot in range(4 * N_COL):
                box = shots[slot]
                whole_area = (box[1:2] - box[0:1]) * (box[3:4] - box[2:3])
                average = (sums[slot, 1:2, :] + sums[slot + N_COL, 0:1, :]) / whole_area
                past = box[4:5]
                doses[slot] = jnp.where(
                    past > 0.0, past * jnp.exp(RELAX * (TARGET_LEVEL - average)), 0.0
                )
        else:
            copy = remote(
                sums_out.at[iteration],
                spill,
                spill_sems.at[0],
                spill_sems.at[1],
                near(-1, c),
            )
            copy.start()
            for other in sent:
                other.wait_send()
            for other in shot_copies:
                other.wait_send()
            for away, other in t_copies:

                @pl.when(away)
                def _(other=other):
                    other.wait_send()

            copy.wait()
            average = (sums_out[iteration, 1:2, :] + spill[0:1, :]) / area
            dose = doses[8 + c]
            dose = jnp.where(live, dose * jnp.exp(RELAX * (TARGET_LEVEL - average)), 0.0)
            dosage_ref[...] = dose.reshape(SLOTS)


def per_device(shot_boxes, shot_counts, shot_doses, transfer):
    t = tables()
    constants = [jnp.asarray(t[name]) for name in NAMES]
    vmem = pl.BlockSpec(memory_space=pltpu.VMEM)
    stay = pl.BlockSpec(memory_space=pl.ANY)
    dma = pltpu.SemaphoreType.DMA
    held = [
        pltpu.VMEM(value.shape[1:] if name == "classes" else value.shape, value.dtype)
        for name, value in zip(NAMES, constants)
    ]
    dosage, exposure = pl.pallas_call(
        kernel,
        out_shape=(
            jax.ShapeDtypeStruct((SLOTS,), F32),
            jax.ShapeDtypeStruct((ROWS, COLS), F32),
        ),
        in_specs=[stay] * (4 + len(constants)),
        out_specs=(vmem, vmem),
        scratch_shapes=[
            *held,
            pltpu.VMEM((4, SLOTS), jnp.int32),
            pltpu.VMEM((1, 1), jnp.int32),
            pltpu.VMEM((1, SLOTS), F32),
            pltpu.VMEM((8, SLOTS), F32),
            pltpu.VMEM((16, 8, SLOTS), F32),
            pltpu.VMEM((16, 1, SLOTS), F32),
            pltpu.VMEM((ITERS, 2, SLOTS), F32),
            pltpu.VMEM((20, 2, SLOTS), F32),
            pltpu.VMEM((2, SLOTS), F32),
            pltpu.VMEM((8, 1, LONG), F32),
            pltpu.VMEM((2, 256, 128), F32),
            pltpu.VMEM((256, 128), F32),
            pltpu.VMEM((4 * SLOTS, COLS), BF16),
            pltpu.VMEM((2, 4 * SLOTS, 128), BF16),
            pltpu.VMEM((N_COL, 2 * SLOTS, 256), BF16),
            pltpu.VMEM((3 * ROWS, 4 * SLOTS), BF16),
            pltpu.VMEM((2, 3 * ROWS, 4 * SLOTS), BF16),
            pltpu.VMEM((ROWS, COLS + 256), BF16),
            pltpu.VMEM((ROWS, COLS), F32),
            pltpu.VMEM((ROWS, COLS), BF16),
            pltpu.VMEM((32, LONG), F32),
            pltpu.VMEM((256, 1024), BF16),
            pltpu.VMEM((ITERS, N_SLAB, 2, 128), BF16),
            pltpu.VMEM((ITERS, N_SLAB, 2, 128), BF16),
            pltpu.VMEM((ITERS, N_SLAB, 2, 128), BF16),
            pltpu.VMEM((ITERS, N_SLAB, 2, 128), BF16),
            pltpu.VMEM((ITERS, N_COL, 32, 1024), BF16),
            pltpu.VMEM((ITERS, N_COL, 32, 1024), BF16),
            dma((len(NAMES),)),
            dma((3,)),
            dma((16,)),
            dma((16,)),
            dma((20,)),
            dma((20,)),
            dma((8,)),
            dma((8,)),
            dma((2 * ITERS,)),
            dma((2 * ITERS,)),
            dma((2 * ITERS,)),
            dma((ITERS, N_COL)),
            dma((ITERS, N_COL)),
            dma((2,)),
        ],
        compiler_params=pltpu.CompilerParams(
            collective_id=0, has_side_effects=True, vmem_limit_bytes=60 << 20
        ),
        name="dose_correction",
    )(shot_boxes, shot_counts, shot_doses.reshape(1, SLOTS), transfer, *constants)
    return dosage, exposure


def solution(mesh):
    placed = (
        P(None, ("slab", "col")),
        P("slab", "col"),
        P(("slab", "col")),
        P(("slab", "col"), None),
    )
    return jax.shard_map(
        per_device,
        mesh=mesh,
        in_specs=placed,
        out_specs=(P(("slab", "col")), P("slab", "col")),
        check_vma=False,
    )
```
